512 devices in a mesh: gx: 8 (over y, core), gy: 16 (over x, z_lo), gz: 4 (over z_hi).
Axes of the slice: x: 4, y: 4, z: 16 (z_hi: 4, z_lo: 4; z = z_hi * 4 + z_lo), core: 2. Of those that a mesh axis runs over, the one named last changes fastest.
Arguments:
- right_side: float32 [128, 256, 1024], P('gz', 'gy', 'gx'), may hold values from -33 to 33
- initial: float32 [128, 256, 1024], P('gz', 'gy', 'gx'), may hold values from -4 to 4
- kappa_sq: float32 [128, 256, 1024], P('gz', 'gy', 'gx'), may hold values from 0.0004 to 4
Outputs:
- solution: float32 [128, 256, 1024], P('gz', 'gy', 'gx')
- residual: float32 [128, 256, 1024], P('gz', 'gy', 'gx')
The draws below stay inside these ranges and needn't reach their ends.
All inputs are finite; a program needn't handle non-finite values.
Results may differ from the reference program's by a relative error of at most 0.0001.
Values sent between devices are 32-bit elements; how exact they have to be, the bound alone decides.
No kernel may reach another device: no remote copies, remote signals or barrier semaphores. Data moves between devices by JAX's collectives and lax.ppermute only.
A program may use at most 64 MiB of HBM per device.

```python
import math
import jax
import jax.numpy as jnp

CX = 128
ITERS = 2
SWEEPS = 3
NX = 1024
NY = 256
NZ = 128


def parity_sign():
    index_z = jnp.arange(NZ, dtype=jnp.int32)[:, None, None]
    index_y = jnp.arange(NY, dtype=jnp.int32)[None, :, None]
    index_x = jnp.arange(NX, dtype=jnp.int32)[None, None, :]
    return (1 - 2 * ((index_z + index_y + index_x) % 2)).astype(jnp.float32)


def band_weight():
    place = jnp.arange(NX, dtype=jnp.int32) % CX
    distance = jnp.minimum(place, CX - 1 - place).astype(jnp.float32)
    return jnp.exp(-(distance / 6.0) * (distance / 6.0))[None, None, :]


def rising_scale():
    along_z = (jnp.arange(NZ, dtype=jnp.float32) / NZ)[:, None, None]
    along_y = (jnp.arange(NY, dtype=jnp.float32) / NY)[None, :, None]
    along_x = (jnp.arange(NX, dtype=jnp.float32) / NX)[None, None, :]
    return jnp.power(3.0, along_z + along_y + along_x)


def draw_right_side(key, part):
    sign_field = parity_sign()
    profile = 0.25 + 0.75 * band_weight()
    scaling = 1.2 * rising_scale()
    factor = jax.random.uniform(key, (NZ, NY, NX), jnp.float32, 0.4, 1.0)
    return jnp.clip(scaling * sign_field * profile * factor, -33.0, 33.0)


def draw_initial(key, part):
    sign_field = parity_sign()
    scaling = 4.0 / 27.0 * rising_scale()
    factor = jax.random.uniform(key, (NZ, NY, NX), jnp.float32, 0.3, 1.0)
    return jnp.clip(-sign_field * scaling * factor, -4.0, 4.0)


def draw_kappa_sq(key, part):
    weight = band_weight()
    floor_band = 0.85
    uniform_draw = jax.random.uniform(key, (NZ, NY, NX), jnp.float32)
    fraction = weight * floor_band + (1.0 - weight * floor_band) * uniform_draw
    values = 0.0004 * jnp.exp(fraction * math.log(10000.0))
    return jnp.clip(values, 0.0004, 4.0)


def setup_inputs(seed: int = 0) -> dict:
    keys = jax.random.split(jax.random.key(seed), 4)
    right_side = draw_right_side(jax.random.fold_in(keys[3], 71), 0)
    initial = draw_initial(jax.random.fold_in(keys[3], 71), 0)
    kappa_sq = draw_kappa_sq(jax.random.fold_in(keys[3], 71), 0)
    return dict(right_side=right_side, initial=initial, kappa_sq=kappa_sq)


cheb_high = 7.2
cheb_low = 0.072


def neighbours(padded):
    total = padded[2:, 1:-1, 1:-1] + padded[:-2, 1:-1, 1:-1]
    total = total + padded[1:-1, 2:, 1:-1] + padded[1:-1, :-2, 1:-1]
    total = total + padded[1:-1, 1:-1, 2:] + padded[1:-1, 1:-1, :-2]
    return total


def apply_k(values, kappa_sq):
    padded = jnp.pad(values, 1)
    return ((6.0 + kappa_sq) * values - neighbours(padded)) / 6.0


def apply_q(values, kappa_sq):
    return apply_k(apply_k(values, kappa_sq), kappa_sq)


def precondition(source, kappa_sq):
    centre = (cheb_high + cheb_low) / 2.0
    half_width = (cheb_high - cheb_low) / 2.0
    ratio_sigma = centre / half_width
    weight_old = 1.0 / ratio_sigma
    update = source / centre
    result = update
    for sweep in range(SWEEPS - 1):
        defect = source - apply_q(result, kappa_sq)
        weight_new = 1.0 / (2.0 * ratio_sigma - weight_old)
        update = weight_new * weight_old * update + (2.0 * weight_new / half_width) * defect
        result = result + update
        weight_old = weight_new
    return result


def reference(right_side, initial, kappa_sq):
    solution = initial
    residual = right_side - apply_q(initial, kappa_sq)
    precond = precondition(residual, kappa_sq)
    direction = precond
    energy = jnp.sum(residual * precond)
    for step in range(ITERS):
        applied = apply_q(direction, kappa_sq)
        step_size = energy / jnp.sum(direction * applied)
        solution = solution + step_size * direction
        residual = residual - step_size * applied
        if step + 1 < ITERS:
            precond = precondition(residual, kappa_sq)
            energy_new = jnp.sum(residual * precond)
            direction = precond + (energy_new / energy) * direction
            energy = energy_new
    return solution, residual
```

```python
import jax
import jax.numpy as jnp
from jax import lax
from jax.experimental import pallas as pl
from jax.experimental.pallas import tpu as pltpu
from jax.sharding import PartitionSpec as P

SWEEPS = 3
HIGH = 7.2
LOW = 0.072

NZ, NY, NX = 32, 16, 128
G = 8
FZ, FY = NZ + 2 * G, NY + 2 * G
DEPTHS = (6, 4, 7)
OFFS = (0, 6, 10)
LAYERS = 17
PIECES = [(f, k) for f in range(3) for k in range(DEPTHS[f])]
MAIN_ROWS = LAYERS * NZ
PACK_ROWS = MAIN_ROWS + LAYERS * 16
Q_PACK = FZ // 16 * FY


def chebyshev():
    centre = (HIGH + LOW) / 2.0
    half = (HIGH - LOW) / 2.0
    sigma = centre / half
    rho = 1.0 / sigma
    d = [1.0 / centre, 0.0, 0.0]
    z = list(d)
    for _ in range(SWEEPS - 1):
        rho_new = 1.0 / (2.0 * sigma - rho)
        defect = [1.0, -z[0], -z[1]]
        d = [rho_new * rho * a + 2.0 * rho_new / half * b for a, b in zip(d, defect)]
        z = [a + b for a, b in zip(z, d)]
        rho = rho_new
    return z


C0, C1, C2 = chebyshev()
SQ = 36.0

f32 = jnp.float32
VM = pl.BlockSpec(memory_space=pltpu.VMEM)


def run(kernel, outs, args, scratch=(), name=None):
    return pl.pallas_call(
        kernel,
        out_shape=[jax.ShapeDtypeStruct(s, f32) for s in outs],
        in_specs=[VM] * len(args),
        out_specs=[VM] * len(outs),
        scratch_shapes=list(scratch),
        name=name,
    )(*args)


def shift(x, axis, step):
    n = lax.axis_size(axis)
    pairs = [(i, i + step) for i in range(n) if 0 <= i + step < n]
    return lax.ppermute(x, axis, pairs)


def exchange(down, up, axis):
    from_above = shift(down, axis, -1)
    from_below = shift(up, axis, 1)
    return from_below, from_above


def pack_y(x_ref, b_ref, k_ref, lo_ref, hi_ref, dn_ref, up_ref):
    fields = (x_ref, b_ref, k_ref)
    for i, (f, k) in enumerate(PIECES):
        d = DEPTHS[f]
        for out, row in ((dn_ref, k), (up_ref, NY - d + k)):
            out[i * NZ : (i + 1) * NZ, :] = fields[f][pl.ds(row, NZ, stride=NY), :]
            at = MAIN_ROWS + i * 16
            first = OFFS[f] * NY + row
            out[at : at + d, :] = lo_ref[pl.ds(first, d, stride=NY), :]
            out[at + 8 : at + 8 + d, :] = hi_ref[pl.ds(first, d, stride=NY), :]


def pack_lanes(read, dn_ref, up_ref, base):
    group = lax.broadcasted_iota(jnp.int32, (FY, NX), 1) // G
    for q in range(FZ // 16):
        dn = jnp.zeros((FY, NX), f32)
        up = jnp.zeros((FY, NX), f32)
        for g in range(16):
            v = read(16 * q + g)
            a = v if g == 0 else pltpu.roll(v, G * g, 1)
            b = v if g == 15 else pltpu.roll(v, G * (g + 1), 1)
            dn = jnp.where(group == g, a, dn)
            up = jnp.where(group == g, b, up)
        dn_ref[base + q * FY : base + (q + 1) * FY, :] = dn
        up_ref[base + q * FY : base + (q + 1) * FY, :] = up


def unpack_lanes(lo_ref, hi_ref, base, write):
    right = lax.broadcasted_iota(jnp.int32, (FY, NX), 1) < NX // 2
    for q in range(FZ // 16):
        lo = lo_ref[base + q * FY : base + (q + 1) * FY, :]
        hi = hi_ref[base + q * FY : base + (q + 1) * FY, :]
        for g in range(16):
            a = hi if g == 0 else pltpu.roll(hi, NX - G * g, 1)
            b = lo if g == 15 else pltpu.roll(lo, NX - G - G * g, 1)
            write(16 * q + g, jnp.where(right, a, b))


def frame(x_ref, b_ref, k_ref, zlo, zhi, ylo, yhi, xe, be, ke, dn_ref, up_ref):
    fields = (x_ref, b_ref, k_ref)
    for f, out in enumerate((xe, be, ke)):
        d = DEPTHS[f]
        out[...] = jnp.zeros((FZ * FY, NX), f32)
        for z in range(NZ):
            at = (G + z) * FY + G
            out[at : at + NY, :] = fields[f][z * NY : (z + 1) * NY, :]
        for j in range(d):
            src = (OFFS[f] + j) * NY
            at = (G - d + j) * FY + G
            out[at : at + NY, :] = zlo[src : src + NY, :]
            at = (G + NZ + j) * FY + G
            out[at : at + NY, :] = zhi[src : src + NY, :]
        for k in range(d):
            i = OFFS[f] + k
            h = MAIN_ROWS + i * 16
            for src, row in ((ylo, G - d + k), (yhi, G + NY + k)):
                out[pl.ds(G * FY + row, NZ, stride=FY), :] = src[i * NZ : (i + 1) * NZ, :]
                out[pl.ds((G - d) * FY + row, d, stride=FY), :] = src[h : h + d, :]
                out[pl.ds((G + NZ) * FY + row, d, stride=FY), :] = src[h + 8 : h + 8 + d, :]
        pack_lanes(lambda z: out[z * FY : (z + 1) * FY, :], dn_ref, up_ref, f * Q_PACK)


def apply_k(src, dst, coef, mask, first, last, finish=None):
    lane = lax.broadcasted_iota(jnp.int32, (FY, NX), 1)
    s0, s1 = src
    c0, c1 = coef
    m0, m1 = mask

    def plane(z, _):
        v0, v1 = s0[z], s1[z]
        a0, a1 = pltpu.roll(v0, 1, 1), pltpu.roll(v1, 1, 1)
        b0, b1 = pltpu.roll(v0, NX - 1, 1), pltpu.roll(v1, NX - 1, 1)
        t0 = jnp.where(lane == 0, a1, a0) + jnp.where(lane == NX - 1, b1, b0)
        t1 = jnp.where(lane == 0, a0, a1) + jnp.where(lane == NX - 1, b0, b1)
        t0 = t0 + pltpu.roll(v0, 1, 0) + pltpu.roll(v0, FY - 1, 0) + s0[z - 1] + s0[z + 1]
        t1 = t1 + pltpu.roll(v1, 1, 0) + pltpu.roll(v1, FY - 1, 0) + s1[z - 1] + s1[z + 1]
        r0 = c0[z] * v0 - m0[z] * t0
        r1 = c1[z] * v1 - m1[z] * t1
        if finish is None:
            dst[0][z] = r0
            dst[1][z] = r1
        else:
            finish(z, r0, r1)
        return 0

    lax.fori_loop(first, last, plane, 0)


def span(radius):
    return G - radius, G + NZ + radius


def first_stage(xe, be, ke, lo, hi, r_out, w_out, wdn, wup, c0, c1, m0, m1, x1, b1, p0, p1, q0, q1):
    def put(ref):
        def write(z, v):
            ref[z] = v

        return write

    def put_coef(z, k1):
        k0 = ke[z]
        c0[z] = 6.0 + k0
        c1[z] = 6.0 + k1
        m0[z] = jnp.where(k0 > 0.0, 1.0, 0.0)
        m1[z] = jnp.where(k1 > 0.0, 1.0, 0.0)

    unpack_lanes(lo, hi, 0, put(x1))
    unpack_lanes(lo, hi, Q_PACK, put(b1))
    unpack_lanes(lo, hi, 2 * Q_PACK, put_coef)
    coef, mask, p, q, b = (c0, c1), (m0, m1), (p0, p1), (q0, q1), (be, b1)

    apply_k((xe, x1), p, coef, mask, *span(5))

    def to_residual(z, v0, v1):
        be[z] = be[z] - v0 * (1.0 / SQ)
        b1[z] = b1[z] - v1 * (1.0 / SQ)

    apply_k(p, None, coef, mask, *span(4), finish=to_residual)
    apply_k(b, p, coef, mask, *span(3))
    apply_k(p, q, coef, mask, *span(2))
    apply_k(q, p, coef, mask, *span(1))

    def to_precond(z, v0, v1):
        w = C0 * be[z] + (C1 / SQ) * q0[z] + (C2 / SQ**2) * v0
        w_out[z - G] = w[G : G + NY, :]
        r_out[z - G] = be[z][G : G + NY, :]

    apply_k(p, None, coef, mask, *span(0), finish=to_precond)
    wdn[...] = w_out[0:G]
    wup[...] = w_out[NZ - G : NZ]


def pack_y2(w_ref, lo_ref, hi_ref, dn_ref, up_ref):
    dn_ref[0:G] = lo_ref[:, 0:G, :]
    up_ref[0:G] = lo_ref[:, NY - G : NY, :]
    dn_ref[G : G + NZ] = w_ref[:, 0:G, :]
    up_ref[G : G + NZ] = w_ref[:, NY - G : NY, :]
    dn_ref[G + NZ : FZ] = hi_ref[:, 0:G, :]
    up_ref[G + NZ : FZ] = hi_ref[:, NY - G : NY, :]


def frame2(w_ref, zlo, zhi, ylo, yhi, we, dn_ref, up_ref):
    we[0:G, G : G + NY, :] = zlo[...]
    we[G : G + NZ, G : G + NY, :] = w_ref[...]
    we[G + NZ : FZ, G : G + NY, :] = zhi[...]
    we[:, 0:G, :] = ylo[...]
    we[:, G + NY : FY, :] = yhi[...]
    pack_lanes(lambda z: we[z], dn_ref, up_ref, 0)


def second_stage(we, lo, hi, r_ref, c0, c1, m0, m1, v1_out, v2_out, v3_out, dots, w1, p0, p1, q0, q1, s0, s1):
    def write(z, v):
        w1[z] = v

    unpack_lanes(lo, hi, 0, write)
    coef, mask, p, q, s = (c0, c1), (m0, m1), (p0, p1), (q0, q1), (s0, s1)
    apply_k((we, w1), p, coef, mask, *span(7))
    apply_k(p, q, coef, mask, *span(6))
    apply_k(q, p, coef, mask, *span(5))
    apply_k(p, s, coef, mask, *span(4))
    apply_k(s, p, coef, mask, *span(3))

    def to_w2(z, a0, a1):
        s0[z] = C0 * q0[z] + (C1 / SQ) * s0[z] + (C2 / SQ**2) * a0
        s1[z] = C0 * q1[z] + (C1 / SQ) * s1[z] + (C2 / SQ**2) * a1

    apply_k(p, None, coef, mask, *span(2), finish=to_w2)
    apply_k(s, p, coef, mask, *span(1))
    dots[...] = jnp.zeros((32, NX), f32)

    def to_w3(z, a0, a1):
        rows = slice(G, G + NY)
        w = we[z][rows]
        u1 = q0[z][rows]
        u2 = s0[z][rows]
        u3 = a0[rows]
        v1_out[z - G] = u1
        v2_out[z - G] = u2
        v3_out[z - G] = u3
        for i, t in enumerate((r_ref[z - G] * w, w * u1, u1 * u2, u2 * u3)):
            dots[8 * i : 8 * i + 8, :] += t[0:8] + t[8:16]

    apply_k(p, None, coef, mask, *span(0), finish=to_w3)


def finish(x_ref, r_ref, w_ref, v1, v2, v3, dots, x_out, r_out):
    def total(i, scale):
        return jnp.sum(dots[8 * i : 8 * i + 8, :], keepdims=True) * (1.0 / scale)

    e0 = total(0, 1.0)
    g0 = total(1, SQ)
    h = total(2, SQ**2)
    k = total(3, SQ**3)
    a0 = e0 / g0
    e1 = a0 * a0 * h - e0
    beta = 1.0 + e1 / e0
    a1 = e1 / (beta * beta * g0 - 2.0 * beta * a0 * h + a0 * a0 * k)
    near = a0 + a1 * beta
    far = a1 * a0
    x_out[...] = x_ref[...] + near[None] * w_ref[...] - (far * (1.0 / SQ))[None] * v2[...]
    r_out[...] = r_ref[...] - (near * (1.0 / SQ))[None] * v1[...] + (far * (1.0 / SQ**2))[None] * v3[...]


def all_sum(x):
    for axis in ("gx", "gy"):
        n = lax.axis_size(axis)
        copies = jnp.broadcast_to(x[None], (n, *x.shape))
        x = jnp.sum(lax.all_to_all(copies, axis, 0, 0), axis=0)
    return lax.psum(x, "gz")


def body(right_side, initial, kappa_sq):
    fields = (initial, right_side, kappa_sq)
    flat = [v.reshape(NZ * NY, NX) for v in fields]
    down = jnp.concatenate([v[:d] for v, d in zip(fields, DEPTHS)], axis=0)
    up = jnp.concatenate([v[NZ - d :] for v, d in zip(fields, DEPTHS)], axis=0)
    zlo, zhi = exchange(down, up, "gz")
    zlo, zhi = zlo.reshape(LAYERS * NY, NX), zhi.reshape(LAYERS * NY, NX)
    down, up = run(pack_y, [(PACK_ROWS, NX)] * 2, (*flat, zlo, zhi), name="pack_y")
    ylo, yhi = exchange(down, up, "gy")
    frame_shape = (FZ, FY, NX)
    xe, be, ke, down, up = run(
        frame, [(FZ * FY, NX)] * 3 + [(3 * Q_PACK, NX)] * 2, (*flat, zlo, zhi, ylo, yhi), name="frame"
    )
    xlo, xhi = exchange(down, up, "gx")
    xe, be, ke = (v.reshape(frame_shape) for v in (xe, be, ke))
    tile = pltpu.VMEM(frame_shape, f32)
    block = (NZ, NY, NX)
    slab = (G, NY, NX)

    def stage1(xe, be_in, *rest):
        be = rest[-1]
        be[...] = be_in[...]
        first_stage(xe, be, *rest[:-1])

    r0, w0, down, up, c0, c1, m0, m1 = run(
        stage1,
        [block, block, slab, slab, frame_shape, frame_shape, frame_shape, frame_shape],
        (xe, be, ke, xlo, xhi),
        scratch=[tile] * 7,
        name="first_stage",
    )
    zlo, zhi = exchange(down, up, "gz")
    down, up = run(pack_y2, [(FZ, G, NX)] * 2, (w0, zlo, zhi), name="pack_y2")
    ylo, yhi = exchange(down, up, "gy")
    we, down, up = run(frame2, [frame_shape, (Q_PACK, NX), (Q_PACK, NX)], (w0, zlo, zhi, ylo, yhi), name="frame2")
    xlo, xhi = exchange(down, up, "gx")
    v1, v2, v3, dots = run(
        second_stage,
        [block, block, block, (32, NX)],
        (we, xlo, xhi, r0, c0, c1, m0, m1),
        scratch=[tile] * 7,
        name="second_stage",
    )
    dots = all_sum(dots)
    x, r = run(finish, [block, block], (initial, r0, w0, v1, v2, v3, dots), name="finish")
    return x, r


def solution(mesh):
    spec = P("gz", "gy", "gx")
    return jax.shard_map(body, mesh=mesh, in_specs=(spec,) * 3, out_specs=(spec,) * 2, check_vma=False)
```

```python
import jax
import jax.numpy as jnp
from jax import lax
from jax.experimental import pallas as pl
from jax.experimental.pallas import tpu as pltpu
from jax.sharding import PartitionSpec as P

SWEEPS = 3
HIGH = 7.2
LOW = 0.072

NZ, NY, NX = 32, 16, 128
G = 8
FZ, FY = NZ + 2 * G, NY + 2 * G
DEPTHS = (6, 4, 7)
OFFS = (0, 6, 10)
LAYERS = 17
PIECES = [(f, t) for f in range(3) for t in range(1, DEPTHS[f] + 1)]
MAIN_ROWS = LAYERS * NZ


def place_corners():
    sizes = [(DEPTHS[f] - t, f, t, side) for f, t in PIECES for side in (0, 1)]
    free, at = [], {}
    for n, f, t, side in sorted(sizes, reverse=True):
        if n == 0:
            continue
        for i, used in enumerate(free):
            if used + n <= 8:
                break
        else:
            free.append(0)
            i = len(free) - 1
        at[f, t, side] = MAIN_ROWS + 8 * i + free[i]
        free[i] += n
    return at, MAIN_ROWS + 8 * len(free)


CORNERS, PACK_ROWS = place_corners()
Q_PACK = FZ // 16 * FY


def chebyshev():
    centre = (HIGH + LOW) / 2.0
    half = (HIGH - LOW) / 2.0
    sigma = centre / half
    rho = 1.0 / sigma
    d = [1.0 / centre, 0.0, 0.0]
    z = list(d)
    for _ in range(SWEEPS - 1):
        rho_new = 1.0 / (2.0 * sigma - rho)
        defect = [1.0, -z[0], -z[1]]
        d = [rho_new * rho * a + 2.0 * rho_new / half * b for a, b in zip(d, defect)]
        z = [a + b for a, b in zip(z, d)]
        rho = rho_new
    return z


C0, C1, C2 = chebyshev()
SQ = 36.0

f32 = jnp.float32
VM = pl.BlockSpec(memory_space=pltpu.VMEM)


def run(kernel, outs, args, scratch=(), name=None, mib=16):
    return pl.pallas_call(
        kernel,
        out_shape=[jax.ShapeDtypeStruct(s, f32) for s in outs],
        in_specs=[VM] * len(args),
        out_specs=[VM] * len(outs),
        scratch_shapes=list(scratch),
        compiler_params=pltpu.CompilerParams(vmem_limit_bytes=mib << 20),
        name=name,
    )(*args)


def shift(x, axis, step):
    n = lax.axis_size(axis)
    pairs = [(i, i + step) for i in range(n) if 0 <= i + step < n]
    return lax.ppermute(x, axis, pairs)


def exchange(down, up, axis):
    from_above = shift(down, axis, -1)
    from_below = shift(up, axis, 1)
    return from_below, from_above


def pack_y(x_ref, b_ref, k_ref, lo_ref, hi_ref, dn_ref, up_ref):
    fields = (x_ref, b_ref, k_ref)
    for i, (f, t) in enumerate(PIECES):
        d, n = DEPTHS[f], DEPTHS[f] - t
        for out, row in ((dn_ref, t - 1), (up_ref, NY - t)):
            out[i * NZ : (i + 1) * NZ, :] = fields[f][pl.ds(row, NZ, stride=NY), :]
            if n:
                at = CORNERS[f, t, 0]
                out[at : at + n, :] = lo_ref[pl.ds((OFFS[f] + d - n) * NY + row, n, stride=NY), :]
                at = CORNERS[f, t, 1]
                out[at : at + n, :] = hi_ref[pl.ds(OFFS[f] * NY + row, n, stride=NY), :]


def pack_lanes(read, dn_ref, up_ref, base):
    group = lax.broadcasted_iota(jnp.int32, (FY, NX), 1) // G
    for q in range(FZ // 16):
        dn = jnp.zeros((FY, NX), f32)
        up = jnp.zeros((FY, NX), f32)
        for g in range(16):
            v = read(16 * q + g)
            a = v if g == 0 else pltpu.roll(v, G * g, 1)
            b = v if g == 15 else pltpu.roll(v, G * (g + 1), 1)
            dn = jnp.where(group == g, a, dn)
            up = jnp.where(group == g, b, up)
        dn_ref[base + q * FY : base + (q + 1) * FY, :] = dn
        up_ref[base + q * FY : base + (q + 1) * FY, :] = up


def unpack_lanes(lo_ref, hi_ref, base, write):
    right = lax.broadcasted_iota(jnp.int32, (FY, NX), 1) < NX // 2
    for q in range(FZ // 16):
        lo = lo_ref[base + q * FY : base + (q + 1) * FY, :]
        hi = hi_ref[base + q * FY : base + (q + 1) * FY, :]
        for g in range(16):
            a = hi if g == 0 else pltpu.roll(hi, NX - G * g, 1)
            b = lo if g == 15 else pltpu.roll(lo, NX - G - G * g, 1)
            write(16 * q + g, jnp.where(right, a, b))


def frame(x_ref, b_ref, k_ref, zlo, zhi, ylo, yhi, xe, be, ke, dn_ref, up_ref):
    fields = (x_ref, b_ref, k_ref)
    for f, out in enumerate((xe, be, ke)):
        d = DEPTHS[f]
        out[...] = jnp.zeros((FZ * FY, NX), f32)
        for z in range(NZ):
            at = (G + z) * FY + G
            out[at : at + NY, :] = fields[f][z * NY : (z + 1) * NY, :]
        for j in range(d):
            src = (OFFS[f] + j) * NY
            at = (G - d + j) * FY + G
            out[at : at + NY, :] = zlo[src : src + NY, :]
            at = (G + NZ + j) * FY + G
            out[at : at + NY, :] = zhi[src : src + NY, :]
        for t in range(1, d + 1):
            i, n = OFFS[f] + t - 1, d - t
            for src, row in ((ylo, G - t), (yhi, G + NY + t - 1)):
                out[pl.ds(G * FY + row, NZ, stride=FY), :] = src[i * NZ : (i + 1) * NZ, :]
                if n:
                    at = CORNERS[f, t, 0]
                    out[pl.ds((G - n) * FY + row, n, stride=FY), :] = src[at : at + n, :]
                    at = CORNERS[f, t, 1]
                    out[pl.ds((G + NZ) * FY + row, n, stride=FY), :] = src[at : at + n, :]
        pack_lanes(lambda z: out[z * FY : (z + 1) * FY, :], dn_ref, up_ref, f * Q_PACK)


PLANES = 4


def apply_k(src, dst, coef, mask, first, last, finish=None):
    s0, s1 = src
    c0, c1 = coef
    m0, m1 = mask

    def planes(z, n):
        lane = lax.broadcasted_iota(jnp.int32, (n, FY, NX), 2)
        here, below, above = pl.ds(z, n), pl.ds(z - 1, n), pl.ds(z + 1, n)
        v0, v1 = s0[here], s1[here]
        a0, a1 = pltpu.roll(v0, 1, 2), pltpu.roll(v1, 1, 2)
        b0, b1 = pltpu.roll(v0, NX - 1, 2), pltpu.roll(v1, NX - 1, 2)
        t0 = jnp.where(lane == 0, a1, a0) + jnp.where(lane == NX - 1, b1, b0)
        t1 = jnp.where(lane == 0, a0, a1) + jnp.where(lane == NX - 1, b0, b1)
        t0 = t0 + (pltpu.roll(v0, 1, 1) + pltpu.roll(v0, FY - 1, 1)) + (s0[below] + s0[above])
        t1 = t1 + (pltpu.roll(v1, 1, 1) + pltpu.roll(v1, FY - 1, 1)) + (s1[below] + s1[above])
        r0 = c0[here] * v0 - m0[here] * t0
        r1 = c1[here] * v1 - m1[here] * t1
        if finish is None:
            dst[0][here] = r0
            dst[1][here] = r1
        else:
            finish(z, n, r0, r1)

    count = last - first
    whole = count // PLANES

    def step(i, _):
        planes(first + i * PLANES, PLANES)
        return 0

    lax.fori_loop(0, whole, step, 0)
    if count % PLANES:
        planes(first + whole * PLANES, count % PLANES)


def span(radius):
    return G - radius, G + NZ + radius


def first_stage(xe, be, ke, lo, hi, r_out, w_out, wdn, wup, c0, c1, m0, m1, x1, b1, p0, p1, q0, q1):
    def put(ref):
        def write(z, v):
            ref[z] = v

        return write

    def put_coef(z, k1):
        k0 = ke[z]
        c0[z] = 6.0 + k0
        c1[z] = 6.0 + k1
        m0[z] = jnp.where(k0 > 0.0, 1.0, 0.0)
        m1[z] = jnp.where(k1 > 0.0, 1.0, 0.0)

    unpack_lanes(lo, hi, 0, put(x1))
    unpack_lanes(lo, hi, Q_PACK, put(b1))
    unpack_lanes(lo, hi, 2 * Q_PACK, put_coef)
    coef, mask, p, q, b = (c0, c1), (m0, m1), (p0, p1), (q0, q1), (be, b1)

    apply_k((xe, x1), p, coef, mask, *span(5))

    def to_residual(z, n, v0, v1):
        at = pl.ds(z, n)
        be[at] = be[at] - v0 * (1.0 / SQ)
        b1[at] = b1[at] - v1 * (1.0 / SQ)

    apply_k(p, None, coef, mask, *span(4), finish=to_residual)
    apply_k(b, p, coef, mask, *span(3))
    apply_k(p, q, coef, mask, *span(2))
    apply_k(q, p, coef, mask, *span(1))

    def to_precond(z, n, v0, v1):
        at = pl.ds(z, n)
        r = be[at]
        w = C0 * r + (C1 / SQ) * q0[at] + (C2 / SQ**2) * v0
        w_out[pl.ds(z - G, n)] = w[:, G : G + NY, :]
        r_out[pl.ds(z - G, n)] = r[:, G : G + NY, :]

    apply_k(p, None, coef, mask, *span(0), finish=to_precond)
    wdn[...] = w_out[0:G]
    wup[...] = w_out[NZ - G : NZ]


def pack_y2(w_ref, lo_ref, hi_ref, dn_ref, up_ref):
    dn_ref[0:G] = lo_ref[:, 0:G, :]
    up_ref[0:G] = lo_ref[:, NY - G : NY, :]
    dn_ref[G : G + NZ] = w_ref[:, 0:G, :]
    up_ref[G : G + NZ] = w_ref[:, NY - G : NY, :]
    dn_ref[G + NZ : FZ] = hi_ref[:, 0:G, :]
    up_ref[G + NZ : FZ] = hi_ref[:, NY - G : NY, :]


def frame2(w_ref, zlo, zhi, ylo, yhi, we, dn_ref, up_ref):
    we[0:G, G : G + NY, :] = zlo[...]
    we[G : G + NZ, G : G + NY, :] = w_ref[...]
    we[G + NZ : FZ, G : G + NY, :] = zhi[...]
    we[:, 0:G, :] = ylo[...]
    we[:, G + NY : FY, :] = yhi[...]
    pack_lanes(lambda z: we[z], dn_ref, up_ref, 0)


def second_stage(we, lo, hi, r_ref, c0, c1, m0, m1, v1_out, v2_out, v3_out, dots, acc, w1, p0, p1, q0, q1, s0, s1):
    def write(z, v):
        w1[z] = v

    unpack_lanes(lo, hi, 0, write)
    coef, mask, p, q, s = (c0, c1), (m0, m1), (p0, p1), (q0, q1), (s0, s1)
    apply_k((we, w1), p, coef, mask, *span(7))
    apply_k(p, q, coef, mask, *span(6))
    apply_k(q, p, coef, mask, *span(5))
    apply_k(p, s, coef, mask, *span(4))
    apply_k(s, p, coef, mask, *span(3))

    def to_w2(z, n, a0, a1):
        at = pl.ds(z, n)
        s0[at] = C0 * q0[at] + (C1 / SQ) * s0[at] + (C2 / SQ**2) * a0
        s1[at] = C0 * q1[at] + (C1 / SQ) * s1[at] + (C2 / SQ**2) * a1

    apply_k(p, None, coef, mask, *span(2), finish=to_w2)
    apply_k(s, p, coef, mask, *span(1))
    acc[...] = jnp.zeros((4, G, NX), f32)

    def to_w3(z, n, a0, a1):
        at, to = pl.ds(z, n), pl.ds(z - G, n)
        rows = slice(G, G + NY)
        w = we[at][:, rows]
        u1 = q0[at][:, rows]
        u2 = s0[at][:, rows]
        u3 = a0[:, rows]
        v1_out[to] = u1
        v2_out[to] = u2
        v3_out[to] = u3
        for i, t in enumerate((r_ref[to] * w, w * u1, u1 * u2, u2 * u3)):
            acc[i] += jnp.sum(t[:, 0:8] + t[:, 8:16], axis=0)

    apply_k(p, None, coef, mask, *span(0), finish=to_w3)
    dots[...] = jnp.zeros((G, NX), f32)
    for i in range(4):
        dots[i : i + 1, :] = jnp.sum(acc[i], axis=0, keepdims=True)


def finish(x_ref, r_ref, w_ref, v1, v2, v3, dots, x_out, r_out):
    def total(i, scale):
        return jnp.sum(dots[i : i + 1, :], axis=1, keepdims=True) * (1.0 / scale)

    e0 = total(0, 1.0)
    g0 = total(1, SQ)
    h = total(2, SQ**2)
    k = total(3, SQ**3)
    a0 = e0 / g0
    e1 = a0 * a0 * h - e0
    beta = 1.0 + e1 / e0
    a1 = e1 / (beta * beta * g0 - 2.0 * beta * a0 * h + a0 * a0 * k)
    near = a0 + a1 * beta
    far = a1 * a0
    x_out[...] = x_ref[...] + near[None] * w_ref[...] - (far * (1.0 / SQ))[None] * v2[...]
    r_out[...] = r_ref[...] - (near * (1.0 / SQ))[None] * v1[...] + (far * (1.0 / SQ**2))[None] * v3[...]


def all_sum(x):
    for axis in ("gx", "gy"):
        n = lax.axis_size(axis)
        copies = jnp.broadcast_to(x[None], (n, *x.shape))
        x = jnp.sum(lax.all_to_all(copies, axis, 0, 0), axis=0)
    return lax.psum(x, "gz")


def body(right_side, initial, kappa_sq):
    fields = (initial, right_side, kappa_sq)
    flat = [v.reshape(NZ * NY, NX) for v in fields]
    down = jnp.concatenate([v[:d] for v, d in zip(fields, DEPTHS)], axis=0)
    up = jnp.concatenate([v[NZ - d :] for v, d in zip(fields, DEPTHS)], axis=0)
    zlo, zhi = exchange(down, up, "gz")
    zlo, zhi = zlo.reshape(LAYERS * NY, NX), zhi.reshape(LAYERS * NY, NX)
    down, up = run(pack_y, [(PACK_ROWS, NX)] * 2, (*flat, zlo, zhi), name="pack_y")
    ylo, yhi = exchange(down, up, "gy")
    frame_shape = (FZ, FY, NX)
    xe, be, ke, down, up = run(
        frame, [(FZ * FY, NX)] * 3 + [(3 * Q_PACK, NX)] * 2, (*flat, zlo, zhi, ylo, yhi), name="frame"
    )
    xlo, xhi = exchange(down, up, "gx")
    xe, be, ke = (v.reshape(frame_shape) for v in (xe, be, ke))
    tile = pltpu.VMEM(frame_shape, f32)
    block = (NZ, NY, NX)
    slab = (G, NY, NX)

    def stage1(xe, be_in, *rest):
        be = rest[-1]
        be[...] = be_in[...]
        first_stage(xe, be, *rest[:-1])

    r0, w0, down, up, c0, c1, m0, m1 = run(
        stage1,
        [block, block, slab, slab, frame_shape, frame_shape, frame_shape, frame_shape],
        (xe, be, ke, xlo, xhi),
        scratch=[tile] * 7,
        name="first_stage",
    )
    zlo, zhi = exchange(down, up, "gz")
    down, up = run(pack_y2, [(FZ, G, NX)] * 2, (w0, zlo, zhi), name="pack_y2")
    ylo, yhi = exchange(down, up, "gy")
    we, down, up = run(frame2, [frame_shape, (Q_PACK, NX), (Q_PACK, NX)], (w0, zlo, zhi, ylo, yhi), name="frame2")
    xlo, xhi = exchange(down, up, "gx")
    v1, v2, v3, dots = run(
        second_stage,
        [block, block, block, (G, NX)],
        (we, xlo, xhi, r0, c0, c1, m0, m1),
        scratch=[pltpu.VMEM((4, G, NX), f32)] + [tile] * 7,
        name="second_stage",
    )
    dots = all_sum(dots)
    x, r = run(finish, [block, block], (initial, r0, w0, v1, v2, v3, dots), name="finish")
    return x, r


def solution(mesh):
    spec = P("gz", "gy", "gx")
    return jax.shard_map(body, mesh=mesh, in_specs=(spec,) * 3, out_specs=(spec,) * 2, check_vma=False)
```

```python
import jax
import jax.numpy as jnp
from jax import lax
from jax.experimental import pallas as pl
from jax.experimental.pallas import tpu as pltpu
from jax.sharding import PartitionSpec as P

SWEEPS = 3
HIGH = 7.2
LOW = 0.072

NZ, NY, NX = 32, 16, 128
G = 8
FZ, FY = NZ + 2 * G, NY + 2 * G
DEPTHS = (6, 4, 7)
OFFS = (0, 6, 10)
LAYERS = 17
PIECES = [(f, t) for f in range(3) for t in range(1, DEPTHS[f] + 1)]
MAIN_ROWS = LAYERS * NZ


def place_corners(depths):
    sizes = [(d - t, f, t, side) for f, d in enumerate(depths) for t in range(1, d) for side in (0, 1)]
    free, at = [], {}
    for n, f, t, side in sorted(sizes, reverse=True):
        for i, used in enumerate(free):
            if used + n <= 8:
                break
        else:
            free.append(0)
            i = len(free) - 1
        at[f, t, side] = 8 * i + free[i]
        free[i] += n
    return at, 8 * len(free)


CORNERS, CORNER_ROWS = place_corners(DEPTHS)
CORNERS2, CORNER_ROWS2 = place_corners((G,))
MAIN_ROWS2 = G * NZ
Q_PACK = FZ // 16 * FY


def chebyshev():
    centre = (HIGH + LOW) / 2.0
    half = (HIGH - LOW) / 2.0
    sigma = centre / half
    rho = 1.0 / sigma
    d = [1.0 / centre, 0.0, 0.0]
    z = list(d)
    for _ in range(SWEEPS - 1):
        rho_new = 1.0 / (2.0 * sigma - rho)
        defect = [1.0, -z[0], -z[1]]
        d = [rho_new * rho * a + 2.0 * rho_new / half * b for a, b in zip(d, defect)]
        z = [a + b for a, b in zip(z, d)]
        rho = rho_new
    return z


C0, C1, C2 = chebyshev()
SQ = 36.0

f32 = jnp.float32
VM = pl.BlockSpec(memory_space=pltpu.VMEM)


def run(kernel, outs, args, scratch=(), name=None, mib=16):
    return pl.pallas_call(
        kernel,
        out_shape=[jax.ShapeDtypeStruct(s, f32) for s in outs],
        in_specs=[VM] * len(args),
        out_specs=[VM] * len(outs),
        scratch_shapes=list(scratch),
        compiler_params=pltpu.CompilerParams(vmem_limit_bytes=mib << 20),
        name=name,
    )(*args)


def shift(x, axis, step):
    n = lax.axis_size(axis)
    pairs = [(i, i + step) for i in range(n) if 0 <= i + step < n]
    return lax.ppermute(x, axis, pairs)


def exchange(down, up, axis):
    from_above = shift(down, axis, -1)
    from_below = shift(up, axis, 1)
    return from_below, from_above


def pack_block(x_ref, b_ref, k_ref, zdn, zup, ydn, yup):
    fields = (x_ref, b_ref, k_ref)
    for f, field in enumerate(fields):
        n = DEPTHS[f] * NY
        at = OFFS[f] * NY
        zdn[at : at + n, :] = field[0:n, :]
        zup[at : at + n, :] = field[NZ * NY - n : NZ * NY, :]
    for i, (f, t) in enumerate(PIECES):
        for out, row in ((ydn, t - 1), (yup, NY - t)):
            out[i * NZ : (i + 1) * NZ, :] = fields[f][pl.ds(row, NZ, stride=NY), :]


def pack_corners(lo_ref, hi_ref, dn_ref, up_ref):
    for f, t in PIECES:
        d, n = DEPTHS[f], DEPTHS[f] - t
        for out, row in ((dn_ref, t - 1), (up_ref, NY - t)):
            if n:
                at = CORNERS[f, t, 0]
                out[at : at + n, :] = lo_ref[pl.ds((OFFS[f] + d - n) * NY + row, n, stride=NY), :]
                at = CORNERS[f, t, 1]
                out[at : at + n, :] = hi_ref[pl.ds(OFFS[f] * NY + row, n, stride=NY), :]


def pack_lanes(read, dn_ref, up_ref, base):
    group = lax.broadcasted_iota(jnp.int32, (FY, NX), 1) // G
    for q in range(FZ // 16):
        dn = jnp.zeros((FY, NX), f32)
        up = jnp.zeros((FY, NX), f32)
        for g in range(16):
            v = read(16 * q + g)
            a = v if g == 0 else pltpu.roll(v, G * g, 1)
            b = v if g == 15 else pltpu.roll(v, G * (g + 1), 1)
            dn = jnp.where(group == g, a, dn)
            up = jnp.where(group == g, b, up)
        dn_ref[base + q * FY : base + (q + 1) * FY, :] = dn
        up_ref[base + q * FY : base + (q + 1) * FY, :] = up


def unpack_lanes(lo_ref, hi_ref, base, write):
    right = lax.broadcasted_iota(jnp.int32, (FY, NX), 1) < NX // 2
    for q in range(FZ // 16):
        lo = lo_ref[base + q * FY : base + (q + 1) * FY, :]
        hi = hi_ref[base + q * FY : base + (q + 1) * FY, :]
        for g in range(16):
            a = hi if g == 0 else pltpu.roll(hi, NX - G * g, 1)
            b = lo if g == 15 else pltpu.roll(lo, NX - G - G * g, 1)
            write(16 * q + g, jnp.where(right, a, b))


def frame(x_ref, b_ref, k_ref, zlo, zhi, ylo, yhi, clo, chi, xe, be, ke, dn_ref, up_ref):
    fields = (x_ref, b_ref, k_ref)
    for f, out in enumerate((xe, be, ke)):
        d = DEPTHS[f]
        out[...] = jnp.zeros((FZ * FY, NX), f32)
        for z in range(NZ):
            at = (G + z) * FY + G
            out[at : at + NY, :] = fields[f][z * NY : (z + 1) * NY, :]
        for j in range(d):
            src = (OFFS[f] + j) * NY
            at = (G - d + j) * FY + G
            out[at : at + NY, :] = zlo[src : src + NY, :]
            at = (G + NZ + j) * FY + G
            out[at : at + NY, :] = zhi[src : src + NY, :]
        for t in range(1, d + 1):
            i, n = OFFS[f] + t - 1, d - t
            for src, corner, row in ((ylo, clo, G - t), (yhi, chi, G + NY + t - 1)):
                out[pl.ds(G * FY + row, NZ, stride=FY), :] = src[i * NZ : (i + 1) * NZ, :]
                if n:
                    at = CORNERS[f, t, 0]
                    out[pl.ds((G - n) * FY + row, n, stride=FY), :] = corner[at : at + n, :]
                    at = CORNERS[f, t, 1]
                    out[pl.ds((G + NZ) * FY + row, n, stride=FY), :] = corner[at : at + n, :]
        pack_lanes(lambda z: out[z * FY : (z + 1) * FY, :], dn_ref, up_ref, f * Q_PACK)


PLANES = 8


def rows_of(z, n, shift=0):
    return pl.ds(pl.multiple_of(z * FY, FY) + shift, n * FY)


def apply_k(src, dst, coef, mask, first, last, finish=None):
    s0, s1 = src
    c0, c1 = coef
    m0, m1 = mask

    def plane(z):
        lane = lax.broadcasted_iota(jnp.int32, (FY, NX), 1)

        def around(ref, v, other):
            x = pltpu.roll(jnp.where(lane == NX - 1, other, v), 1, 1)
            x = x + pltpu.roll(jnp.where(lane == 0, other, v), NX - 1, 1)
            y = ref[rows_of(z, 1, -1)] + ref[rows_of(z, 1, 1)]
            return (y + (ref[rows_of(z, 1, -FY)] + ref[rows_of(z, 1, FY)])) + x

        here = rows_of(z, 1)
        v0, v1 = s0[here], s1[here]
        r0 = c0[here] * v0 - m0[here] * around(s0, v0, v1)
        r1 = c1[here] * v1 - m1[here] * around(s1, v1, v0)
        if finish is None:
            dst[0][here] = r0
            dst[1][here] = r1
        else:
            finish(z, 1, r0, r1)

    def planes(z, n):
        for k in range(n):
            plane(z + k)

    count = last - first
    whole = count // PLANES

    def step(i, _):
        planes(first + i * PLANES, PLANES)
        return 0

    lax.fori_loop(0, whole, step, 0)
    if count % PLANES:
        planes(first + whole * PLANES, count % PLANES)


def block_of(v, n):
    return v.reshape(n, FY, NX)[:, G : G + NY]


def span(radius):
    return G - radius, G + NZ + radius


def first_stage(xe, be, ke, lo, hi, r_out, w_out, wdn, wup, c0, c1, m0, m1, x1, b1, p0, p1, q0, q1):
    def put(ref):
        def write(z, v):
            ref[z * FY : (z + 1) * FY] = v

        return write

    def put_coef(z, k1):
        at = slice(z * FY, (z + 1) * FY)
        k0 = ke[at]
        c0[at] = 6.0 + k0
        c1[at] = 6.0 + k1
        m0[at] = jnp.where(k0 > 0.0, 1.0, 0.0)
        m1[at] = jnp.where(k1 > 0.0, 1.0, 0.0)

    unpack_lanes(lo, hi, 0, put(x1))
    unpack_lanes(lo, hi, Q_PACK, put(b1))
    unpack_lanes(lo, hi, 2 * Q_PACK, put_coef)
    coef, mask, p, q, b = (c0, c1), (m0, m1), (p0, p1), (q0, q1), (be, b1)

    apply_k((xe, x1), p, coef, mask, *span(5))

    def to_residual(z, n, v0, v1):
        at = rows_of(z, n)
        be[at] = be[at] - v0 * (1.0 / SQ)
        b1[at] = b1[at] - v1 * (1.0 / SQ)

    apply_k(p, None, coef, mask, *span(4), finish=to_residual)
    apply_k(b, p, coef, mask, *span(3))
    apply_k(p, q, coef, mask, *span(2))
    apply_k(q, p, coef, mask, *span(1))

    def to_precond(z, n, v0, v1):
        at = rows_of(z, n)
        r = be[at]
        w = C0 * r + (C1 / SQ) * q0[at] + (C2 / SQ**2) * v0
        w_out[pl.ds(z - G, n)] = block_of(w, n)
        r_out[pl.ds(z - G, n)] = block_of(r, n)

    apply_k(p, None, coef, mask, *span(0), finish=to_precond)
    wdn[...] = w_out[0:G]
    wup[...] = w_out[NZ - G : NZ]


def pack_y2(w_ref, lo_ref, hi_ref, dn_ref, up_ref):
    for t in range(1, G + 1):
        n = G - t
        for out, row in ((dn_ref, t - 1), (up_ref, NY - t)):
            out[(t - 1) * NZ : t * NZ, :] = w_ref[pl.ds(row, NZ, stride=NY), :]
            if n:
                at = MAIN_ROWS2 + CORNERS2[0, t, 0]
                out[at : at + n, :] = lo_ref[pl.ds(t * NY + row, n, stride=NY), :]
                at = MAIN_ROWS2 + CORNERS2[0, t, 1]
                out[at : at + n, :] = hi_ref[pl.ds(row, n, stride=NY), :]


def frame2(w_ref, zlo, zhi, ylo, yhi, we, dn_ref, up_ref):
    for z in range(FZ):
        at = z * FY
        src, k = (zlo, z) if z < G else (w_ref, z - G) if z < G + NZ else (zhi, z - G - NZ)
        we[at + G : at + G + NY, :] = src[k * NY : (k + 1) * NY, :]
        if z < G or z >= G + NZ:
            we[at : at + G, :] = jnp.zeros((G, NX), f32)
            we[at + G + NY : at + FY, :] = jnp.zeros((G, NX), f32)
    for t in range(1, G + 1):
        n = G - t
        for src, row in ((ylo, G - t), (yhi, G + NY + t - 1)):
            we[pl.ds(G * FY + row, NZ, stride=FY), :] = src[(t - 1) * NZ : t * NZ, :]
            if n:
                at = MAIN_ROWS2 + CORNERS2[0, t, 0]
                we[pl.ds((G - n) * FY + row, n, stride=FY), :] = src[at : at + n, :]
                at = MAIN_ROWS2 + CORNERS2[0, t, 1]
                we[pl.ds((G + NZ) * FY + row, n, stride=FY), :] = src[at : at + n, :]
    pack_lanes(lambda z: we[z * FY : (z + 1) * FY, :], dn_ref, up_ref, 0)


def second_stage(we, lo, hi, r_ref, c0, c1, m0, m1, v1_out, v2_out, v3_out, dots, acc, w1, p0, p1, q0, q1, s0, s1):
    def write(z, v):
        w1[z * FY : (z + 1) * FY] = v

    unpack_lanes(lo, hi, 0, write)
    coef, mask, p, q, s = (c0, c1), (m0, m1), (p0, p1), (q0, q1), (s0, s1)
    apply_k((we, w1), p, coef, mask, *span(7))
    apply_k(p, q, coef, mask, *span(6))
    apply_k(q, p, coef, mask, *span(5))
    apply_k(p, s, coef, mask, *span(4))
    apply_k(s, p, coef, mask, *span(3))

    def to_w2(z, n, a0, a1):
        at = rows_of(z, n)
        s0[at] = C0 * q0[at] + (C1 / SQ) * s0[at] + (C2 / SQ**2) * a0
        s1[at] = C0 * q1[at] + (C1 / SQ) * s1[at] + (C2 / SQ**2) * a1

    apply_k(p, None, coef, mask, *span(2), finish=to_w2)
    apply_k(s, p, coef, mask, *span(1))
    acc[...] = jnp.zeros((4, G, NX), f32)

    def to_w3(z, n, a0, a1):
        at, to = rows_of(z, n), pl.ds(z - G, n)
        w, u1, u2, u3 = (block_of(v, n) for v in (we[at], q0[at], s0[at], a0))
        v1_out[to] = u1
        v2_out[to] = u2
        v3_out[to] = u3
        for i, t in enumerate((r_ref[to] * w, w * u1, u1 * u2, u2 * u3)):
            acc[i] += jnp.sum(t[:, 0:8] + t[:, 8:16], axis=0)

    apply_k(p, None, coef, mask, *span(0), finish=to_w3)
    dots[...] = jnp.zeros((G, NX), f32)
    for i in range(4):
        dots[i : i + 1, :] = jnp.sum(acc[i], axis=0, keepdims=True)


def finish(x_ref, r_ref, w_ref, v1, v2, v3, dots, x_out, r_out):
    def total(i, scale):
        return jnp.sum(dots[i : i + 1, :], axis=1, keepdims=True) * (1.0 / scale)

    e0 = total(0, 1.0)
    g0 = total(1, SQ)
    h = total(2, SQ**2)
    k = total(3, SQ**3)
    a0 = e0 / g0
    e1 = a0 * a0 * h - e0
    beta = 1.0 + e1 / e0
    a1 = e1 / (beta * beta * g0 - 2.0 * beta * a0 * h + a0 * a0 * k)
    near = a0 + a1 * beta
    far = a1 * a0
    x_out[...] = x_ref[...] + near[None] * w_ref[...] - (far * (1.0 / SQ))[None] * v2[...]
    r_out[...] = r_ref[...] - (near * (1.0 / SQ))[None] * v1[...] + (far * (1.0 / SQ**2))[None] * v3[...]


def all_sum(x):
    for axis in ("gx", "gy"):
        n = lax.axis_size(axis)
        copies = jnp.broadcast_to(x[None], (n, *x.shape))
        x = jnp.sum(lax.all_to_all(copies, axis, 0, 0), axis=0)
    return lax.psum(x, "gz")


def body(right_side, initial, kappa_sq):
    flat = [v.reshape(NZ * NY, NX) for v in (initial, right_side, kappa_sq)]
    zdn, zup, ydn, yup = run(
        pack_block, [(LAYERS * NY, NX)] * 2 + [(MAIN_ROWS, NX)] * 2, flat, name="pack_block"
    )
    ylo, yhi = exchange(ydn, yup, "gy")
    zlo, zhi = exchange(zdn, zup, "gz")
    down, up = run(pack_corners, [(CORNER_ROWS, NX)] * 2, (zlo, zhi), name="pack_corners")
    clo, chi = exchange(down, up, "gy")
    frame_shape = (FZ * FY, NX)
    xe, be, ke, down, up = run(
        frame, [frame_shape] * 3 + [(3 * Q_PACK, NX)] * 2, (*flat, zlo, zhi, ylo, yhi, clo, chi), name="frame"
    )
    xlo, xhi = exchange(down, up, "gx")
    tile = pltpu.VMEM(frame_shape, f32)
    block = (NZ, NY, NX)
    slab = (G, NY, NX)

    def stage1(xe, be_in, *rest):
        be = rest[-1]
        be[...] = be_in[...]
        first_stage(xe, be, *rest[:-1])

    r0, w0, down, up, c0, c1, m0, m1 = run(
        stage1,
        [block, block, slab, slab, frame_shape, frame_shape, frame_shape, frame_shape],
        (xe, be, ke, xlo, xhi),
        scratch=[tile] * 7,
        name="first_stage",
    )
    zlo, zhi = exchange(down, up, "gz")
    w_flat, zlo, zhi = (v.reshape(-1, NX) for v in (w0, zlo, zhi))
    down, up = run(pack_y2, [(MAIN_ROWS2 + CORNER_ROWS2, NX)] * 2, (w_flat, zlo, zhi), name="pack_y2")
    ylo, yhi = exchange(down, up, "gy")
    we, down, up = run(frame2, [frame_shape, (Q_PACK, NX), (Q_PACK, NX)], (w_flat, zlo, zhi, ylo, yhi), name="frame2")
    xlo, xhi = exchange(down, up, "gx")
    v1, v2, v3, dots = run(
        second_stage,
        [block, block, block, (G, NX)],
        (we, xlo, xhi, r0, c0, c1, m0, m1),
        scratch=[pltpu.VMEM((4, G, NX), f32)] + [tile] * 7,
        name="second_stage",
    )
    dots = all_sum(dots)
    x, r = run(finish, [block, block], (initial, r0, w0, v1, v2, v3, dots), name="finish")
    return x, r


def solution(mesh):
    spec = P("gz", "gy", "gx")
    return jax.shard_map(body, mesh=mesh, in_specs=(spec,) * 3, out_specs=(spec,) * 2, check_vma=False)
```

```python
import jax
import jax.numpy as jnp
from jax import lax
from jax.experimental import pallas as pl
from jax.experimental.pallas import tpu as pltpu
from jax.sharding import PartitionSpec as P

SWEEPS = 3
HIGH = 7.2
LOW = 0.072

NZ, NY, NX = 32, 16, 128
G = 8
FZ, FY = NZ + 2 * G, NY + 2 * G
DEPTHS = (6, 4, 7)
OFFS = (0, 6, 10)
LAYERS = 17
PIECES = [(f, t) for f in range(3) for t in range(1, DEPTHS[f] + 1)]
MAIN_ROWS = LAYERS * NZ


def place_corners(depths):
    sizes = [(d - t, f, t, side) for f, d in enumerate(depths) for t in range(1, d) for side in (0, 1)]
    free, at = [], {}
    for n, f, t, side in sorted(sizes, reverse=True):
        for i, used in enumerate(free):
            if used + n <= 8:
                break
        else:
            free.append(0)
            i = len(free) - 1
        at[f, t, side] = 8 * i + free[i]
        free[i] += n
    return at, 8 * len(free)


CORNERS, CORNER_ROWS = place_corners(DEPTHS)
CORNERS2, CORNER_ROWS2 = place_corners((G,))
MAIN_ROWS2 = G * NZ
Q_PACK = FZ // 16 * FY


def chebyshev():
    centre = (HIGH + LOW) / 2.0
    half = (HIGH - LOW) / 2.0
    sigma = centre / half
    rho = 1.0 / sigma
    d = [1.0 / centre, 0.0, 0.0]
    z = list(d)
    for _ in range(SWEEPS - 1):
        rho_new = 1.0 / (2.0 * sigma - rho)
        defect = [1.0, -z[0], -z[1]]
        d = [rho_new * rho * a + 2.0 * rho_new / half * b for a, b in zip(d, defect)]
        z = [a + b for a, b in zip(z, d)]
        rho = rho_new
    return z


C0, C1, C2 = chebyshev()
SQ = 36.0

f32 = jnp.float32
VM = pl.BlockSpec(memory_space=pltpu.VMEM)


def run(kernel, outs, args, scratch=(), mib=16, space=pltpu.VMEM):
    return pl.pallas_call(
        kernel,
        out_shape=[jax.ShapeDtypeStruct(s, f32) for s in outs],
        in_specs=[pl.BlockSpec(memory_space=space)] * len(args),
        out_specs=[VM] * len(outs),
        scratch_shapes=list(scratch),
        compiler_params=pltpu.CompilerParams(vmem_limit_bytes=mib << 20),
    )(*args)


def shift(x, axis, step):
    n = lax.axis_size(axis)
    pairs = [(i, i + step) for i in range(n) if 0 <= i + step < n]
    return lax.ppermute(x, axis, pairs)


def exchange(down, up, axis):
    from_above = shift(down, axis, -1)
    from_below = shift(up, axis, 1)
    return from_below, from_above


def pack_block(x_hbm, b_hbm, k_hbm, zdn, zup, ydn, yup, x_ref, b_ref, k_ref, sems):
    fields = (x_ref, b_ref, k_ref)
    copies = [
        pltpu.make_async_copy(src, dst, sems.at[i])
        for i, (src, dst) in enumerate(zip((x_hbm, b_hbm, k_hbm), fields))
    ]
    for copy in copies:
        copy.start()
    for copy in copies:
        copy.wait()
    for f, field in enumerate(fields):
        n = DEPTHS[f] * NY
        at = OFFS[f] * NY
        zdn[at : at + n, :] = field[0:n, :]
        zup[at : at + n, :] = field[NZ * NY - n : NZ * NY, :]
    for i, (f, t) in enumerate(PIECES):
        for out, row in ((ydn, t - 1), (yup, NY - t)):
            out[i * NZ : (i + 1) * NZ, :] = fields[f][pl.ds(row, NZ, stride=NY), :]


def pack_corners(lo_ref, hi_ref, dn_ref, up_ref):
    for f, t in PIECES:
        d, n = DEPTHS[f], DEPTHS[f] - t
        for out, row in ((dn_ref, t - 1), (up_ref, NY - t)):
            if n:
                at = CORNERS[f, t, 0]
                out[at : at + n, :] = lo_ref[pl.ds((OFFS[f] + d - n) * NY + row, n, stride=NY), :]
                at = CORNERS[f, t, 1]
                out[at : at + n, :] = hi_ref[pl.ds(OFFS[f] * NY + row, n, stride=NY), :]


def pack_lanes(read, dn_ref, up_ref, base):
    group = lax.broadcasted_iota(jnp.int32, (FY, NX), 1) // G
    for q in range(FZ // 16):
        dn = jnp.zeros((FY, NX), f32)
        up = jnp.zeros((FY, NX), f32)
        for g in range(16):
            v = read(16 * q + g)
            a = v if g == 0 else pltpu.roll(v, G * g, 1)
            b = v if g == 15 else pltpu.roll(v, G * (g + 1), 1)
            dn = jnp.where(group == g, a, dn)
            up = jnp.where(group == g, b, up)
        dn_ref[base + q * FY : base + (q + 1) * FY, :] = dn
        up_ref[base + q * FY : base + (q + 1) * FY, :] = up


def unpack_lanes(lo_ref, hi_ref, base, write):
    right = lax.broadcasted_iota(jnp.int32, (FY, NX), 1) < NX // 2
    for q in range(FZ // 16):
        lo = lo_ref[base + q * FY : base + (q + 1) * FY, :]
        hi = hi_ref[base + q * FY : base + (q + 1) * FY, :]
        for g in range(16):
            a = hi if g == 0 else pltpu.roll(hi, NX - G * g, 1)
            b = lo if g == 15 else pltpu.roll(lo, NX - G - G * g, 1)
            write(16 * q + g, jnp.where(right, a, b))


def frame(x_ref, b_ref, k_ref, zlo, zhi, ylo, yhi, clo, chi, xe, be, ke, dn_ref, up_ref):
    fields = (x_ref, b_ref, k_ref)
    for f, out in enumerate((xe, be, ke)):
        d = DEPTHS[f]
        out[...] = jnp.zeros((FZ * FY, NX), f32)
        for z in range(NZ):
            at = (G + z) * FY + G
            out[at : at + NY, :] = fields[f][z * NY : (z + 1) * NY, :]
        for j in range(d):
            src = (OFFS[f] + j) * NY
            at = (G - d + j) * FY + G
            out[at : at + NY, :] = zlo[src : src + NY, :]
            at = (G + NZ + j) * FY + G
            out[at : at + NY, :] = zhi[src : src + NY, :]
        for t in range(1, d + 1):
            i, n = OFFS[f] + t - 1, d - t
            for src, corner, row in ((ylo, clo, G - t), (yhi, chi, G + NY + t - 1)):
                out[pl.ds(G * FY + row, NZ, stride=FY), :] = src[i * NZ : (i + 1) * NZ, :]
                if n:
                    at = CORNERS[f, t, 0]
                    out[pl.ds((G - n) * FY + row, n, stride=FY), :] = corner[at : at + n, :]
                    at = CORNERS[f, t, 1]
                    out[pl.ds((G + NZ) * FY + row, n, stride=FY), :] = corner[at : at + n, :]
        pack_lanes(lambda z: out[z * FY : (z + 1) * FY, :], dn_ref, up_ref, f * Q_PACK)


PLANES = 8


def rows_of(z, n, shift=0):
    return pl.ds(pl.multiple_of(z * FY, FY) + shift, n * FY)


def apply_k(src, dst, coef, mask, first, last, finish=None):
    s0, s1 = src
    c0, c1 = coef
    m0, m1 = mask

    def plane(z):
        lane = lax.broadcasted_iota(jnp.int32, (FY, NX), 1)

        def around(ref, v, other):
            x = pltpu.roll(jnp.where(lane == NX - 1, other, v), 1, 1)
            x = x + pltpu.roll(jnp.where(lane == 0, other, v), NX - 1, 1)
            y = ref[rows_of(z, 1, -1)] + ref[rows_of(z, 1, 1)]
            return (y + (ref[rows_of(z, 1, -FY)] + ref[rows_of(z, 1, FY)])) + x

        here = rows_of(z, 1)
        v0, v1 = s0[here], s1[here]
        r0 = c0[here] * v0 - m0[here] * around(s0, v0, v1)
        r1 = c1[here] * v1 - m1[here] * around(s1, v1, v0)
        if finish is None:
            dst[0][here] = r0
            dst[1][here] = r1
        else:
            finish(z, 1, r0, r1)

    def planes(z, n):
        for k in range(n):
            plane(z + k)

    count = last - first
    whole = count // PLANES

    def step(i, _):
        planes(first + i * PLANES, PLANES)
        return 0

    lax.fori_loop(0, whole, step, 0)
    if count % PLANES:
        planes(first + whole * PLANES, count % PLANES)


def block_of(v, n):
    return v.reshape(n, FY, NX)[:, G : G + NY]


def span(radius):
    return G - radius, G + NZ + radius


def first_stage(xe, be, ke, lo, hi, r_out, w_out, wdn, wup, c0, c1, m0, m1, x1, b1, p0, p1, q0, q1):
    def put(ref):
        def write(z, v):
            ref[z * FY : (z + 1) * FY] = v

        return write

    def put_coef(z, k1):
        at = slice(z * FY, (z + 1) * FY)
        k0 = ke[at]
        c0[at] = 6.0 + k0
        c1[at] = 6.0 + k1
        m0[at] = jnp.where(k0 > 0.0, 1.0, 0.0)
        m1[at] = jnp.where(k1 > 0.0, 1.0, 0.0)

    unpack_lanes(lo, hi, 0, put(x1))
    unpack_lanes(lo, hi, Q_PACK, put(b1))
    unpack_lanes(lo, hi, 2 * Q_PACK, put_coef)
    coef, mask, p, q, b = (c0, c1), (m0, m1), (p0, p1), (q0, q1), (be, b1)

    apply_k((xe, x1), p, coef, mask, *span(5))

    def to_residual(z, n, v0, v1):
        at = rows_of(z, n)
        be[at] = be[at] - v0 * (1.0 / SQ)
        b1[at] = b1[at] - v1 * (1.0 / SQ)

    apply_k(p, None, coef, mask, *span(4), finish=to_residual)
    apply_k(b, p, coef, mask, *span(3))
    apply_k(p, q, coef, mask, *span(2))
    apply_k(q, p, coef, mask, *span(1))

    def to_precond(z, n, v0, v1):
        at = rows_of(z, n)
        r = be[at]
        w = C0 * r + (C1 / SQ) * q0[at] + (C2 / SQ**2) * v0
        w_out[pl.ds(z - G, n)] = block_of(w, n)
        r_out[pl.ds(z - G, n)] = block_of(r, n)

    apply_k(p, None, coef, mask, *span(0), finish=to_precond)
    wdn[...] = w_out[0:G]
    wup[...] = w_out[NZ - G : NZ]


def pack_y2(w_ref, lo_ref, hi_ref, dn_ref, up_ref):
    for t in range(1, G + 1):
        n = G - t
        for out, row in ((dn_ref, t - 1), (up_ref, NY - t)):
            out[(t - 1) * NZ : t * NZ, :] = w_ref[pl.ds(row, NZ, stride=NY), :]
            if n:
                at = MAIN_ROWS2 + CORNERS2[0, t, 0]
                out[at : at + n, :] = lo_ref[pl.ds(t * NY + row, n, stride=NY), :]
                at = MAIN_ROWS2 + CORNERS2[0, t, 1]
                out[at : at + n, :] = hi_ref[pl.ds(row, n, stride=NY), :]


def frame2(w_ref, zlo, zhi, ylo, yhi, we, dn_ref, up_ref):
    for z in range(FZ):
        at = z * FY
        src, k = (zlo, z) if z < G else (w_ref, z - G) if z < G + NZ else (zhi, z - G - NZ)
        we[at + G : at + G + NY, :] = src[k * NY : (k + 1) * NY, :]
        if z < G or z >= G + NZ:
            we[at : at + G, :] = jnp.zeros((G, NX), f32)
            we[at + G + NY : at + FY, :] = jnp.zeros((G, NX), f32)
    for t in range(1, G + 1):
        n = G - t
        for src, row in ((ylo, G - t), (yhi, G + NY + t - 1)):
            we[pl.ds(G * FY + row, NZ, stride=FY), :] = src[(t - 1) * NZ : t * NZ, :]
            if n:
                at = MAIN_ROWS2 + CORNERS2[0, t, 0]
                we[pl.ds((G - n) * FY + row, n, stride=FY), :] = src[at : at + n, :]
                at = MAIN_ROWS2 + CORNERS2[0, t, 1]
                we[pl.ds((G + NZ) * FY + row, n, stride=FY), :] = src[at : at + n, :]
    pack_lanes(lambda z: we[z * FY : (z + 1) * FY, :], dn_ref, up_ref, 0)


def second_stage(we, lo, hi, r_ref, c0, c1, m0, m1, v1_out, v2_out, v3_out, dots, acc, w1, p0, p1, q0, q1, s0, s1):
    def write(z, v):
        w1[z * FY : (z + 1) * FY] = v

    unpack_lanes(lo, hi, 0, write)
    coef, mask, p, q, s = (c0, c1), (m0, m1), (p0, p1), (q0, q1), (s0, s1)
    apply_k((we, w1), p, coef, mask, *span(7))
    apply_k(p, q, coef, mask, *span(6))
    apply_k(q, p, coef, mask, *span(5))
    apply_k(p, s, coef, mask, *span(4))
    apply_k(s, p, coef, mask, *span(3))

    def to_w2(z, n, a0, a1):
        at = rows_of(z, n)
        s0[at] = C0 * q0[at] + (C1 / SQ) * s0[at] + (C2 / SQ**2) * a0
        s1[at] = C0 * q1[at] + (C1 / SQ) * s1[at] + (C2 / SQ**2) * a1

    apply_k(p, None, coef, mask, *span(2), finish=to_w2)
    apply_k(s, p, coef, mask, *span(1))
    acc[...] = jnp.zeros((4, G, NX), f32)

    def to_w3(z, n, a0, a1):
        at, to = rows_of(z, n), pl.ds(z - G, n)
        w, u1, u2, u3 = (block_of(v, n) for v in (we[at], q0[at], s0[at], a0))
        v1_out[to] = u1
        v2_out[to] = u2
        v3_out[to] = u3
        for i, t in enumerate((r_ref[to] * w, w * u1, u1 * u2, u2 * u3)):
            acc[i] += jnp.sum(t[:, 0:8] + t[:, 8:16], axis=0)

    apply_k(p, None, coef, mask, *span(0), finish=to_w3)
    dots[...] = jnp.zeros((G, NX), f32)
    for i in range(4):
        dots[i : i + 1, :] = jnp.sum(acc[i], axis=0, keepdims=True)


def finish(x_ref, r_ref, w_ref, v1, v2, v3, dots, x_out, r_out):
    def total(i, scale):
        return jnp.sum(dots[i : i + 1, :], axis=1, keepdims=True) * (1.0 / scale)

    e0 = total(0, 1.0)
    g0 = total(1, SQ)
    h = total(2, SQ**2)
    k = total(3, SQ**3)
    a0 = e0 / g0
    e1 = a0 * a0 * h - e0
    beta = 1.0 + e1 / e0
    a1 = e1 / (beta * beta * g0 - 2.0 * beta * a0 * h + a0 * a0 * k)
    near = a0 + a1 * beta
    far = a1 * a0
    x_out[...] = x_ref[...] + near[None] * w_ref[...] - (far * (1.0 / SQ))[None] * v2[...]
    r_out[...] = r_ref[...] - (near * (1.0 / SQ))[None] * v1[...] + (far * (1.0 / SQ**2))[None] * v3[...]


def all_sum(x):
    for axis in ("gx", "gy"):
        n = lax.axis_size(axis)
        copies = jnp.broadcast_to(x[None], (n, *x.shape))
        x = jnp.sum(lax.all_to_all(copies, axis, 0, 0), axis=0)
    return lax.psum(x, "gz")


def solve(right_side, initial, kappa_sq):
    flat = [v.reshape(NZ * NY, NX) for v in (initial, right_side, kappa_sq)]
    zdn, zup, ydn, yup = run(
        pack_block,
        [(LAYERS * NY, NX)] * 2 + [(MAIN_ROWS, NX)] * 2,
        [pltpu.with_memory_space_constraint(v, pltpu.HBM) for v in flat],
        scratch=[pltpu.VMEM((NZ * NY, NX), f32)] * 3 + [pltpu.SemaphoreType.DMA((3,))],
        space=pltpu.HBM,
    )
    zlo, zhi = exchange(zdn, zup, "gz")
    ylo, yhi = exchange(ydn, yup, "gy")
    down, up = run(pack_corners, [(CORNER_ROWS, NX)] * 2, (zlo, zhi))
    clo, chi = exchange(down, up, "gy")
    frame_shape = (FZ * FY, NX)
    xe, be, ke, down, up = run(frame, [frame_shape] * 3 + [(3 * Q_PACK, NX)] * 2, (*flat, zlo, zhi, ylo, yhi, clo, chi))
    xlo, xhi = exchange(down, up, "gx")
    tile = pltpu.VMEM(frame_shape, f32)
    block = (NZ, NY, NX)
    slab = (G, NY, NX)

    def stage1(xe, be_in, *rest):
        be = rest[-1]
        be[...] = be_in[...]
        first_stage(xe, be, *rest[:-1])

    r0, w0, down, up, c0, c1, m0, m1 = run(
        stage1,
        [block, block, slab, slab, frame_shape, frame_shape, frame_shape, frame_shape],
        (xe, be, ke, xlo, xhi),
        scratch=[tile] * 7,
    )
    zlo, zhi = exchange(down, up, "gz")
    w_flat, zlo, zhi = (v.reshape(-1, NX) for v in (w0, zlo, zhi))
    down, up = run(pack_y2, [(MAIN_ROWS2 + CORNER_ROWS2, NX)] * 2, (w_flat, zlo, zhi))
    ylo, yhi = exchange(down, up, "gy")
    we, down, up = run(frame2, [frame_shape, (Q_PACK, NX), (Q_PACK, NX)], (w_flat, zlo, zhi, ylo, yhi))
    xlo, xhi = exchange(down, up, "gx")
    v1, v2, v3, dots = run(
        second_stage,
        [block, block, block, (G, NX)],
        (we, xlo, xhi, r0, c0, c1, m0, m1),
        scratch=[pltpu.VMEM((4, G, NX), f32)] + [tile] * 7,
    )
    dots = all_sum(dots)
    x, r = run(finish, [block, block], (initial, r0, w0, v1, v2, v3, dots))
    return x, r


def solution(mesh):
    spec = P("gz", "gy", "gx")
    return jax.shard_map(solve, mesh=mesh, in_specs=(spec,) * 3, out_specs=(spec,) * 2, check_vma=False)
```

```python
import jax
import jax.numpy as jnp
from jax import lax
from jax.experimental import pallas as pl
from jax.experimental.pallas import tpu as pltpu
from jax.sharding import PartitionSpec as P

SWEEPS = 3
HIGH = 7.2
LOW = 0.072

NZ, NY, NX = 32, 16, 128
G = 8
FZ, FY = NZ + 2 * G, NY + 2 * G
DEPTHS = (6, 4, 7)
OFFS = (0, 6, 10)
LAYERS = 17
PIECES = [(f, t) for f in range(3) for t in range(1, DEPTHS[f] + 1)]
MAIN_ROWS = LAYERS * NZ


def place_corners(depths):
    sizes = [(d - t, f, t, side) for f, d in enumerate(depths) for t in range(1, d) for side in (0, 1)]
    free, at = [], {}
    for n, f, t, side in sorted(sizes, reverse=True):
        for i, used in enumerate(free):
            if used + n <= 8:
                break
        else:
            free.append(0)
            i = len(free) - 1
        at[f, t, side] = 8 * i + free[i]
        free[i] += n
    return at, 8 * len(free)


CORNERS, CORNER_ROWS = place_corners(DEPTHS)
CORNERS2, CORNER_ROWS2 = place_corners((G,))
MAIN_ROWS2 = G * NZ
Q_PACK = FZ // 16 * FY


def chebyshev():
    centre = (HIGH + LOW) / 2.0
    half = (HIGH - LOW) / 2.0
    sigma = centre / half
    rho = 1.0 / sigma
    d = [1.0 / centre, 0.0, 0.0]
    z = list(d)
    for _ in range(SWEEPS - 1):
        rho_new = 1.0 / (2.0 * sigma - rho)
        defect = [1.0, -z[0], -z[1]]
        d = [rho_new * rho * a + 2.0 * rho_new / half * b for a, b in zip(d, defect)]
        z = [a + b for a, b in zip(z, d)]
        rho = rho_new
    return z


C0, C1, C2 = chebyshev()
SQ = 36.0

f32 = jnp.float32
VM = pl.BlockSpec(memory_space=pltpu.VMEM)


def run(kernel, outs, args, scratch=(), mib=16, space=pltpu.VMEM):
    return pl.pallas_call(
        kernel,
        out_shape=[jax.ShapeDtypeStruct(s, f32) for s in outs],
        in_specs=[pl.BlockSpec(memory_space=space)] * len(args),
        out_specs=[VM] * len(outs),
        scratch_shapes=list(scratch),
        compiler_params=pltpu.CompilerParams(vmem_limit_bytes=mib << 20),
    )(*args)


def shift(x, axis, step):
    n = lax.axis_size(axis)
    pairs = [(i, i + step) for i in range(n) if 0 <= i + step < n]
    return lax.ppermute(x, axis, pairs)


def exchange(down, up, axis):
    from_above = shift(down, axis, -1)
    from_below = shift(up, axis, 1)
    return from_below, from_above


def pack_block(x_hbm, b_hbm, k_hbm, zdn, zup, ydn, yup, x_ref, b_ref, k_ref, sems):
    fields = (x_ref, b_ref, k_ref)
    copies = [
        pltpu.make_async_copy(src, dst, sems.at[i])
        for i, (src, dst) in enumerate(zip((x_hbm, b_hbm, k_hbm), fields))
    ]
    for copy in copies:
        copy.start()
    for copy in copies:
        copy.wait()
    for f, field in enumerate(fields):
        n = DEPTHS[f] * NY
        at = OFFS[f] * NY
        zdn[at : at + n, :] = field[0:n, :]
        zup[at : at + n, :] = field[NZ * NY - n : NZ * NY, :]
    for i, (f, t) in enumerate(PIECES):
        for out, row in ((ydn, t - 1), (yup, NY - t)):
            out[i * NZ : (i + 1) * NZ, :] = fields[f][pl.ds(row, NZ, stride=NY), :]


def pack_corners(lo_ref, hi_ref, dn_ref, up_ref):
    for f, t in PIECES:
        d, n = DEPTHS[f], DEPTHS[f] - t
        for out, row in ((dn_ref, t - 1), (up_ref, NY - t)):
            if n:
                at = CORNERS[f, t, 0]
                out[at : at + n, :] = lo_ref[pl.ds((OFFS[f] + d - n) * NY + row, n, stride=NY), :]
                at = CORNERS[f, t, 1]
                out[at : at + n, :] = hi_ref[pl.ds(OFFS[f] * NY + row, n, stride=NY), :]


def pack_lanes(read, dn_ref, up_ref, base):
    group = lax.broadcasted_iota(jnp.int32, (FY, NX), 1) // G
    for q in range(FZ // 16):
        dn = jnp.zeros((FY, NX), f32)
        up = jnp.zeros((FY, NX), f32)
        for g in range(16):
            v = read(16 * q + g)
            a = v if g == 0 else pltpu.roll(v, G * g, 1)
            dn = jnp.where(group == g, a, dn)
            up = jnp.where(group == (g - 1) % 16, a, up)
        dn_ref[base + q * FY : base + (q + 1) * FY, :] = dn
        up_ref[base + q * FY : base + (q + 1) * FY, :] = up


def unpack_lanes(lo_ref, hi_ref, base, write):
    group = lax.broadcasted_iota(jnp.int32, (FY, NX), 1) // G
    for q in range(FZ // 16):
        lo = lo_ref[base + q * FY : base + (q + 1) * FY, :]
        hi = hi_ref[base + q * FY : base + (q + 1) * FY, :]
        for g in range(16):
            v = jnp.where(group == g, hi, lo)
            write(16 * q + g, v if g == 0 else pltpu.roll(v, NX - G * g, 1))


def frame(x_ref, b_ref, k_ref, zlo, zhi, ylo, yhi, clo, chi, xe, be, ke, dn_ref, up_ref):
    fields = (x_ref, b_ref, k_ref)
    for f, out in enumerate((xe, be, ke)):
        d = DEPTHS[f]
        out[...] = jnp.zeros((FZ * FY, NX), f32)
        for z in range(NZ):
            at = (G + z) * FY + G
            out[at : at + NY, :] = fields[f][z * NY : (z + 1) * NY, :]
        for j in range(d):
            src = (OFFS[f] + j) * NY
            at = (G - d + j) * FY + G
            out[at : at + NY, :] = zlo[src : src + NY, :]
            at = (G + NZ + j) * FY + G
            out[at : at + NY, :] = zhi[src : src + NY, :]
        for t in range(1, d + 1):
            i, n = OFFS[f] + t - 1, d - t
            for src, corner, row in ((ylo, clo, G - t), (yhi, chi, G + NY + t - 1)):
                out[pl.ds(G * FY + row, NZ, stride=FY), :] = src[i * NZ : (i + 1) * NZ, :]
                if n:
                    at = CORNERS[f, t, 0]
                    out[pl.ds((G - n) * FY + row, n, stride=FY), :] = corner[at : at + n, :]
                    at = CORNERS[f, t, 1]
                    out[pl.ds((G + NZ) * FY + row, n, stride=FY), :] = corner[at : at + n, :]
        pack_lanes(lambda z: out[z * FY : (z + 1) * FY, :], dn_ref, up_ref, f * Q_PACK)


PLANES = 8


def rows_of(z, n, shift=0):
    return pl.ds(pl.multiple_of(z * FY, FY) + shift, n * FY)


def apply_k(src, dst, coef, mask, first, last, finish=None):
    s0, s1 = src
    c0, c1 = coef
    m0, m1 = mask

    def plane(z):
        lane = lax.broadcasted_iota(jnp.int32, (FY, NX), 1)

        def around(ref, v, other):
            x = pltpu.roll(jnp.where(lane == NX - 1, other, v), 1, 1)
            x = x + pltpu.roll(jnp.where(lane == 0, other, v), NX - 1, 1)
            y = ref[rows_of(z, 1, -1)] + ref[rows_of(z, 1, 1)]
            return (y + (ref[rows_of(z, 1, -FY)] + ref[rows_of(z, 1, FY)])) + x

        here = rows_of(z, 1)
        v0, v1 = s0[here], s1[here]
        r0 = c0[here] * v0 - m0[here] * around(s0, v0, v1)
        r1 = c1[here] * v1 - m1[here] * around(s1, v1, v0)
        if finish is None:
            dst[0][here] = r0
            dst[1][here] = r1
        else:
            finish(z, 1, r0, r1)

    def planes(z, n):
        for k in range(n):
            plane(z + k)

    count = last - first
    whole = count // PLANES

    def step(i, _):
        planes(first + i * PLANES, PLANES)
        return 0

    lax.fori_loop(0, whole, step, 0)
    if count % PLANES:
        planes(first + whole * PLANES, count % PLANES)


def block_of(v, n):
    return v.reshape(n, FY, NX)[:, G : G + NY].reshape(n * NY, NX)


def block_rows(z, n):
    return pl.ds(pl.multiple_of((z - G) * NY, NY), n * NY)


def span(radius):
    return G - radius, G + NZ + radius


def first_stage(xe, be, ke, lo, hi, r_out, w_out, zdn, zup, ydn, yup, c0, c1, m0, m1, x1, b1, p0, p1, q0, q1):
    def put(ref):
        def write(z, v):
            ref[z * FY : (z + 1) * FY] = v

        return write

    def put_coef(z, k1):
        at = slice(z * FY, (z + 1) * FY)
        k0 = ke[at]
        c0[at] = 6.0 + k0
        c1[at] = 6.0 + k1
        m0[at] = jnp.where(k0 > 0.0, 1.0, 0.0)
        m1[at] = jnp.where(k1 > 0.0, 1.0, 0.0)

    unpack_lanes(lo, hi, 0, put(x1))
    unpack_lanes(lo, hi, Q_PACK, put(b1))
    unpack_lanes(lo, hi, 2 * Q_PACK, put_coef)
    coef, mask, p, q, b = (c0, c1), (m0, m1), (p0, p1), (q0, q1), (be, b1)

    apply_k((xe, x1), p, coef, mask, *span(5))

    def to_residual(z, n, v0, v1):
        at = rows_of(z, n)
        be[at] = be[at] - v0 * (1.0 / SQ)
        b1[at] = b1[at] - v1 * (1.0 / SQ)

    apply_k(p, None, coef, mask, *span(4), finish=to_residual)
    apply_k(b, p, coef, mask, *span(3))
    apply_k(p, q, coef, mask, *span(2))
    apply_k(q, p, coef, mask, *span(1))

    def to_precond(z, n, v0, v1):
        at = rows_of(z, n)
        r = be[at]
        w = C0 * r + (C1 / SQ) * q0[at] + (C2 / SQ**2) * v0
        w_out[block_rows(z, n)] = block_of(w, n)
        r_out[block_rows(z, n)] = block_of(r, n)

    apply_k(p, None, coef, mask, *span(0), finish=to_precond)
    zdn[...] = w_out[0 : G * NY]
    zup[...] = w_out[(NZ - G) * NY : NZ * NY]
    for t in range(1, G + 1):
        ydn[(t - 1) * NZ : t * NZ, :] = w_out[pl.ds(t - 1, NZ, stride=NY), :]
        yup[(t - 1) * NZ : t * NZ, :] = w_out[pl.ds(NY - t, NZ, stride=NY), :]


def pack_corners2(lo_ref, hi_ref, dn_ref, up_ref):
    for t in range(1, G):
        n = G - t
        for out, row in ((dn_ref, t - 1), (up_ref, NY - t)):
            at = CORNERS2[0, t, 0]
            out[at : at + n, :] = lo_ref[pl.ds(t * NY + row, n, stride=NY), :]
            at = CORNERS2[0, t, 1]
            out[at : at + n, :] = hi_ref[pl.ds(row, n, stride=NY), :]


def frame2(w_ref, zlo, zhi, ylo, yhi, clo, chi, we, dn_ref, up_ref):
    for z in range(FZ):
        at = z * FY
        src, k = (zlo, z) if z < G else (w_ref, z - G) if z < G + NZ else (zhi, z - G - NZ)
        we[at + G : at + G + NY, :] = src[k * NY : (k + 1) * NY, :]
        if z < G or z >= G + NZ:
            we[at : at + G, :] = jnp.zeros((G, NX), f32)
            we[at + G + NY : at + FY, :] = jnp.zeros((G, NX), f32)
    for t in range(1, G + 1):
        n = G - t
        for src, corner, row in ((ylo, clo, G - t), (yhi, chi, G + NY + t - 1)):
            we[pl.ds(G * FY + row, NZ, stride=FY), :] = src[(t - 1) * NZ : t * NZ, :]
            if n:
                at = CORNERS2[0, t, 0]
                we[pl.ds((G - n) * FY + row, n, stride=FY), :] = corner[at : at + n, :]
                at = CORNERS2[0, t, 1]
                we[pl.ds((G + NZ) * FY + row, n, stride=FY), :] = corner[at : at + n, :]
    pack_lanes(lambda z: we[z * FY : (z + 1) * FY, :], dn_ref, up_ref, 0)


def second_stage(we, lo, hi, r_ref, c0, c1, m0, m1, v1_out, v2_out, v3_out, dots, acc, w1, p0, p1, q0, q1, s0, s1):
    def write(z, v):
        w1[z * FY : (z + 1) * FY] = v

    unpack_lanes(lo, hi, 0, write)
    coef, mask, p, q, s = (c0, c1), (m0, m1), (p0, p1), (q0, q1), (s0, s1)
    apply_k((we, w1), p, coef, mask, *span(7))
    apply_k(p, q, coef, mask, *span(6))
    apply_k(q, p, coef, mask, *span(5))
    apply_k(p, s, coef, mask, *span(4))
    apply_k(s, p, coef, mask, *span(3))

    def to_w2(z, n, a0, a1):
        at = rows_of(z, n)
        s0[at] = C0 * q0[at] + (C1 / SQ) * s0[at] + (C2 / SQ**2) * a0
        s1[at] = C0 * q1[at] + (C1 / SQ) * s1[at] + (C2 / SQ**2) * a1

    apply_k(p, None, coef, mask, *span(2), finish=to_w2)
    apply_k(s, p, coef, mask, *span(1))
    acc[...] = jnp.zeros((4, G, NX), f32)

    def to_w3(z, n, a0, a1):
        at, to = rows_of(z, n), block_rows(z, n)
        w, u1, u2, u3 = (block_of(v, n) for v in (we[at], q0[at], s0[at], a0))
        v1_out[to] = u1
        v2_out[to] = u2
        v3_out[to] = u3
        for i, t in enumerate((r_ref[to] * w, w * u1, u1 * u2, u2 * u3)):
            acc[i] += jnp.sum(t.reshape(n * NY // G, G, NX), axis=0)

    apply_k(p, None, coef, mask, *span(0), finish=to_w3)
    dots[...] = jnp.zeros((G, NX), f32)
    for i in range(4):
        dots[i : i + 1, :] = jnp.sum(acc[i], axis=0, keepdims=True)


def finish(x_ref, r_ref, w_ref, v1, v2, v3, dots, x_out, r_out):
    def total(i, scale):
        return jnp.sum(dots[i : i + 1, :], axis=1, keepdims=True) * (1.0 / scale)

    e0 = total(0, 1.0)
    g0 = total(1, SQ)
    h = total(2, SQ**2)
    k = total(3, SQ**3)
    a0 = e0 / g0
    e1 = a0 * a0 * h - e0
    beta = 1.0 + e1 / e0
    a1 = e1 / (beta * beta * g0 - 2.0 * beta * a0 * h + a0 * a0 * k)
    near = a0 + a1 * beta
    far = a1 * a0
    x_out[...] = x_ref[...] + near * w_ref[...] - (far * (1.0 / SQ)) * v2[...]
    r_out[...] = r_ref[...] - (near * (1.0 / SQ)) * v1[...] + (far * (1.0 / SQ**2)) * v3[...]


def all_sum(x):
    for axis in ("gx", "gy"):
        n = lax.axis_size(axis)
        copies = jnp.broadcast_to(x[None], (n, *x.shape))
        x = jnp.sum(lax.all_to_all(copies, axis, 0, 0), axis=0)
    return lax.psum(x, "gz")


def solve(right_side, initial, kappa_sq):
    flat = [v.reshape(NZ * NY, NX) for v in (initial, right_side, kappa_sq)]
    zdn, zup, ydn, yup = run(
        pack_block,
        [(LAYERS * NY, NX)] * 2 + [(MAIN_ROWS, NX)] * 2,
        [pltpu.with_memory_space_constraint(v, pltpu.HBM) for v in flat],
        scratch=[pltpu.VMEM((NZ * NY, NX), f32)] * 3 + [pltpu.SemaphoreType.DMA((3,))],
        space=pltpu.HBM,
    )
    zlo, zhi = exchange(zdn, zup, "gz")
    ylo, yhi = exchange(ydn, yup, "gy")
    down, up = run(pack_corners, [(CORNER_ROWS, NX)] * 2, (zlo, zhi))
    clo, chi = exchange(down, up, "gy")
    frame_shape = (FZ * FY, NX)
    xe, be, ke, down, up = run(frame, [frame_shape] * 3 + [(3 * Q_PACK, NX)] * 2, (*flat, zlo, zhi, ylo, yhi, clo, chi))
    xlo, xhi = exchange(down, up, "gx")
    tile = pltpu.VMEM(frame_shape, f32)
    block = (NZ * NY, NX)
    slab = (G * NY, NX)

    def stage1(xe, be_in, *rest):
        be = rest[-1]
        be[...] = be_in[...]
        first_stage(xe, be, *rest[:-1])

    r0, w0, zdn, zup, ydn, yup, c0, c1, m0, m1 = run(
        stage1,
        [block, block, slab, slab, (MAIN_ROWS2, NX), (MAIN_ROWS2, NX), frame_shape, frame_shape, frame_shape, frame_shape],
        (xe, be, ke, xlo, xhi),
        scratch=[tile] * 7,
    )
    zlo, zhi = exchange(zdn, zup, "gz")
    ylo, yhi = exchange(ydn, yup, "gy")
    down, up = run(pack_corners2, [(CORNER_ROWS2, NX)] * 2, (zlo, zhi))
    clo, chi = exchange(down, up, "gy")
    we, down, up = run(frame2, [frame_shape, (Q_PACK, NX), (Q_PACK, NX)], (w0, zlo, zhi, ylo, yhi, clo, chi))
    xlo, xhi = exchange(down, up, "gx")
    v1, v2, v3, dots = run(
        second_stage,
        [block, block, block, (G, NX)],
        (we, xlo, xhi, r0, c0, c1, m0, m1),
        scratch=[pltpu.VMEM((4, G, NX), f32)] + [tile] * 7,
    )
    dots = all_sum(dots)
    x, r = run(finish, [block, block], (flat[0], r0, w0, v1, v2, v3, dots))
    return x.reshape(NZ, NY, NX), r.reshape(NZ, NY, NX)


def solution(mesh):
    spec = P("gz", "gy", "gx")
    return jax.shard_map(solve, mesh=mesh, in_specs=(spec,) * 3, out_specs=(spec,) * 2, check_vma=False)
```

```python
import jax
import jax.numpy as jnp
from jax import lax
from jax.experimental import pallas as pl
from jax.experimental.pallas import tpu as pltpu
from jax.sharding import PartitionSpec as P

SWEEPS = 3
HIGH = 7.2
LOW = 0.072

NZ, NY, NX = 32, 16, 128
G = 8
FZ, FY = NZ + 2 * G, NY + 2 * G
DEPTHS = (6, 4, 7)
OFFS = (0, 6, 10)
LAYERS = 17
PIECES = [(f, t) for f in range(3) for t in range(1, DEPTHS[f] + 1)]
MAIN_ROWS = LAYERS * NZ


def place_corners(depths):
    sizes = [(d - t, f, t, side) for f, d in enumerate(depths) for t in range(1, d) for side in (0, 1)]
    free, at = [], {}
    for n, f, t, side in sorted(sizes, reverse=True):
        for i, used in enumerate(free):
            if used + n <= 8:
                break
        else:
            free.append(0)
            i = len(free) - 1
        at[f, t, side] = 8 * i + free[i]
        free[i] += n
    return at, 8 * len(free)


CORNERS, CORNER_ROWS = place_corners(DEPTHS)
CORNERS2, CORNER_ROWS2 = place_corners((G,))
MAIN_ROWS2 = G * NZ
Q_PACK = FZ // 16 * FY


def chebyshev():
    centre = (HIGH + LOW) / 2.0
    half = (HIGH - LOW) / 2.0
    sigma = centre / half
    rho = 1.0 / sigma
    d = [1.0 / centre, 0.0, 0.0]
    z = list(d)
    for _ in range(SWEEPS - 1):
        rho_new = 1.0 / (2.0 * sigma - rho)
        defect = [1.0, -z[0], -z[1]]
        d = [rho_new * rho * a + 2.0 * rho_new / half * b for a, b in zip(d, defect)]
        z = [a + b for a, b in zip(z, d)]
        rho = rho_new
    return z


C0, C1, C2 = chebyshev()
SQ = 36.0

f32 = jnp.float32
VM = pl.BlockSpec(memory_space=pltpu.VMEM)


def run(kernel, outs, args, scratch=(), mib=16, space=pltpu.VMEM):
    return pl.pallas_call(
        kernel,
        out_shape=[jax.ShapeDtypeStruct(s, f32) for s in outs],
        in_specs=[pl.BlockSpec(memory_space=space)] * len(args),
        out_specs=[VM] * len(outs),
        scratch_shapes=list(scratch),
        compiler_params=pltpu.CompilerParams(vmem_limit_bytes=mib << 20),
    )(*args)


def shift(x, axis, step):
    n = lax.axis_size(axis)
    pairs = [(i, i + step) for i in range(n) if 0 <= i + step < n]
    return lax.ppermute(x, axis, pairs)


def exchange(down, up, axis):
    from_above = shift(down, axis, -1)
    from_below = shift(up, axis, 1)
    return from_below, from_above


def pack_block(x_hbm, b_hbm, k_hbm, zdn, zup, ydn, yup, x_ref, b_ref, k_ref, sems):
    fields = (x_ref, b_ref, k_ref)
    copies = [
        pltpu.make_async_copy(src, dst, sems.at[i])
        for i, (src, dst) in enumerate(zip((x_hbm, b_hbm, k_hbm), fields))
    ]
    for copy in copies:
        copy.start()
    for copy in copies:
        copy.wait()
    for f, field in enumerate(fields):
        n = DEPTHS[f] * NY
        at = OFFS[f] * NY
        zdn[at : at + n, :] = field[0:n, :]
        zup[at : at + n, :] = field[NZ * NY - n : NZ * NY, :]
    for i, (f, t) in enumerate(PIECES):
        for out, row in ((ydn, t - 1), (yup, NY - t)):
            out[i * NZ : (i + 1) * NZ, :] = fields[f][pl.ds(row, NZ, stride=NY), :]


def pack_corners(lo_ref, hi_ref, dn_ref, up_ref):
    for f, t in PIECES:
        d, n = DEPTHS[f], DEPTHS[f] - t
        for out, row in ((dn_ref, t - 1), (up_ref, NY - t)):
            if n:
                at = CORNERS[f, t, 0]
                out[at : at + n, :] = lo_ref[pl.ds((OFFS[f] + d - n) * NY + row, n, stride=NY), :]
                at = CORNERS[f, t, 1]
                out[at : at + n, :] = hi_ref[pl.ds(OFFS[f] * NY + row, n, stride=NY), :]


def pack_lanes(read, dn_ref, up_ref, base):
    group = lax.broadcasted_iota(jnp.int32, (FY, NX), 1) // G
    for q in range(FZ // 16):
        dn = jnp.zeros((FY, NX), f32)
        up = jnp.zeros((FY, NX), f32)
        for g in range(16):
            v = read(16 * q + g)
            a = v if g == 0 else pltpu.roll(v, G * g, 1)
            dn = jnp.where(group == g, a, dn)
            up = jnp.where(group == (g - 1) % 16, a, up)
        dn_ref[base + q * FY : base + (q + 1) * FY, :] = dn
        up_ref[base + q * FY : base + (q + 1) * FY, :] = up


def unpack_lanes(lo_ref, hi_ref, base, write):
    group = lax.broadcasted_iota(jnp.int32, (FY, NX), 1) // G
    for q in range(FZ // 16):
        lo = lo_ref[base + q * FY : base + (q + 1) * FY, :]
        hi = hi_ref[base + q * FY : base + (q + 1) * FY, :]
        for g in range(16):
            v = jnp.where(group == g, hi, lo)
            write(16 * q + g, v if g == 0 else pltpu.roll(v, NX - G * g, 1))


def frame(x_ref, b_ref, k_ref, zlo, zhi, ylo, yhi, clo, chi, xe, be, ke, dn_ref, up_ref):
    fields = (x_ref, b_ref, k_ref)
    for f, out in enumerate((xe, be, ke)):
        d = DEPTHS[f]
        out[...] = jnp.zeros((FZ * FY, NX), f32)
        for z in range(NZ):
            at = (G + z) * FY + G
            out[at : at + NY, :] = fields[f][z * NY : (z + 1) * NY, :]
        for j in range(d):
            src = (OFFS[f] + j) * NY
            at = (G - d + j) * FY + G
            out[at : at + NY, :] = zlo[src : src + NY, :]
            at = (G + NZ + j) * FY + G
            out[at : at + NY, :] = zhi[src : src + NY, :]
        for t in range(1, d + 1):
            i, n = OFFS[f] + t - 1, d - t
            for src, corner, row in ((ylo, clo, G - t), (yhi, chi, G + NY + t - 1)):
                out[pl.ds(G * FY + row, NZ, stride=FY), :] = src[i * NZ : (i + 1) * NZ, :]
                if n:
                    at = CORNERS[f, t, 0]
                    out[pl.ds((G - n) * FY + row, n, stride=FY), :] = corner[at : at + n, :]
                    at = CORNERS[f, t, 1]
                    out[pl.ds((G + NZ) * FY + row, n, stride=FY), :] = corner[at : at + n, :]
        pack_lanes(lambda z: out[z * FY : (z + 1) * FY, :], dn_ref, up_ref, f * Q_PACK)


PLANES = 8
GROUP = 4


class Window:
    def __init__(self, radius):
        self.first, self.last = G - radius, G + NZ + radius
        self.y, self.n = (G, NY) if radius == 0 else (4, 24) if radius <= 4 else (0, FY)

    def at(self, z, shift=0):
        return pl.ds(pl.multiple_of(z * FY, FY) + (self.y + shift), self.n)


def apply_k(src, dst, coef, mask, radius, finish=None):
    win = Window(radius)
    s0, s1 = src
    c0, c1 = coef
    m0, m1 = mask

    def group(planes):
        lane = lax.broadcasted_iota(jnp.int32, (win.n, NX), 1)
        here = [win.at(z) for z in planes]
        v0, v1 = [s0[at] for at in here], [s1[at] for at in here]
        left0 = [pltpu.roll(jnp.where(lane == NX - 1, b, a), 1, 1) for a, b in zip(v0, v1)]
        left1 = [pltpu.roll(jnp.where(lane == NX - 1, a, b), 1, 1) for a, b in zip(v0, v1)]
        right0 = [pltpu.roll(jnp.where(lane == 0, b, a), NX - 1, 1) for a, b in zip(v0, v1)]
        right1 = [pltpu.roll(jnp.where(lane == 0, a, b), NX - 1, 1) for a, b in zip(v0, v1)]

        def around(ref, z):
            y = ref[win.at(z, -1)] + ref[win.at(z, 1)]
            return y + (ref[win.at(z, -FY)] + ref[win.at(z, FY)])

        for i, z in enumerate(planes):
            at = here[i]
            r0 = c0[at] * v0[i] - m0[at] * (around(s0, z) + (left0[i] + right0[i]))
            r1 = c1[at] * v1[i] - m1[at] * (around(s1, z) + (left1[i] + right1[i]))
            if finish is None:
                dst[0][at] = r0
                dst[1][at] = r1
            else:
                finish(z, at, r0, r1)

    def some(z, n):
        for k in range(0, n, GROUP):
            group([z + k + i for i in range(min(GROUP, n - k))])

    count = win.last - win.first
    whole = count // PLANES

    def step(i, _):
        some(win.first + i * PLANES, PLANES)
        return 0

    lax.fori_loop(0, whole, step, 0)
    if count % PLANES:
        some(win.first + whole * PLANES, count % PLANES)


def block_rows(z):
    return pl.ds(pl.multiple_of((z - G) * NY, NY), NY)


def first_stage(xe, be, ke, lo, hi, r_out, w_out, zdn, zup, ydn, yup, c0, c1, m0, m1, x1, b1, p0, p1, q0, q1):
    def put(ref):
        def write(z, v):
            ref[z * FY : (z + 1) * FY] = v

        return write

    def put_coef(z, k1):
        at = slice(z * FY, (z + 1) * FY)
        k0 = ke[at]
        c0[at] = 6.0 + k0
        c1[at] = 6.0 + k1
        m0[at] = jnp.where(k0 > 0.0, 1.0, 0.0)
        m1[at] = jnp.where(k1 > 0.0, 1.0, 0.0)

    unpack_lanes(lo, hi, 0, put(x1))
    unpack_lanes(lo, hi, Q_PACK, put(b1))
    unpack_lanes(lo, hi, 2 * Q_PACK, put_coef)
    coef, mask, p, q, b = (c0, c1), (m0, m1), (p0, p1), (q0, q1), (be, b1)

    apply_k((xe, x1), p, coef, mask, 5)

    def to_residual(z, at, v0, v1):
        be[at] = be[at] - v0 * (1.0 / SQ)
        b1[at] = b1[at] - v1 * (1.0 / SQ)

    apply_k(p, None, coef, mask, 4, finish=to_residual)
    apply_k(b, p, coef, mask, 3)
    apply_k(p, q, coef, mask, 2)
    apply_k(q, p, coef, mask, 1)

    def to_precond(z, at, v0, _):
        r = be[at]
        w_out[block_rows(z)] = C0 * r + (C1 / SQ) * q0[at] + (C2 / SQ**2) * v0
        r_out[block_rows(z)] = r

    apply_k(p, None, coef, mask, 0, finish=to_precond)
    zdn[...] = w_out[0 : G * NY]
    zup[...] = w_out[(NZ - G) * NY : NZ * NY]
    for t in range(1, G + 1):
        ydn[(t - 1) * NZ : t * NZ, :] = w_out[pl.ds(t - 1, NZ, stride=NY), :]
        yup[(t - 1) * NZ : t * NZ, :] = w_out[pl.ds(NY - t, NZ, stride=NY), :]


def pack_corners2(lo_ref, hi_ref, dn_ref, up_ref):
    for t in range(1, G):
        n = G - t
        for out, row in ((dn_ref, t - 1), (up_ref, NY - t)):
            at = CORNERS2[0, t, 0]
            out[at : at + n, :] = lo_ref[pl.ds(t * NY + row, n, stride=NY), :]
            at = CORNERS2[0, t, 1]
            out[at : at + n, :] = hi_ref[pl.ds(row, n, stride=NY), :]


def frame2(w_ref, zlo, zhi, ylo, yhi, clo, chi, we, dn_ref, up_ref):
    for z in range(FZ):
        at = z * FY
        src, k = (zlo, z) if z < G else (w_ref, z - G) if z < G + NZ else (zhi, z - G - NZ)
        we[at + G : at + G + NY, :] = src[k * NY : (k + 1) * NY, :]
        if z < G or z >= G + NZ:
            we[at : at + G, :] = jnp.zeros((G, NX), f32)
            we[at + G + NY : at + FY, :] = jnp.zeros((G, NX), f32)
    for t in range(1, G + 1):
        n = G - t
        for src, corner, row in ((ylo, clo, G - t), (yhi, chi, G + NY + t - 1)):
            we[pl.ds(G * FY + row, NZ, stride=FY), :] = src[(t - 1) * NZ : t * NZ, :]
            if n:
                at = CORNERS2[0, t, 0]
                we[pl.ds((G - n) * FY + row, n, stride=FY), :] = corner[at : at + n, :]
                at = CORNERS2[0, t, 1]
                we[pl.ds((G + NZ) * FY + row, n, stride=FY), :] = corner[at : at + n, :]
    pack_lanes(lambda z: we[z * FY : (z + 1) * FY, :], dn_ref, up_ref, 0)


def second_stage(we, lo, hi, r_ref, c0, c1, m0, m1, v1_out, v2_out, v3_out, dots, acc, w1, p0, p1, q0, q1, s0, s1):
    def write(z, v):
        w1[z * FY : (z + 1) * FY] = v

    unpack_lanes(lo, hi, 0, write)
    coef, mask, p, q, s = (c0, c1), (m0, m1), (p0, p1), (q0, q1), (s0, s1)
    apply_k((we, w1), p, coef, mask, 7)
    apply_k(p, q, coef, mask, 6)
    apply_k(q, p, coef, mask, 5)
    apply_k(p, s, coef, mask, 4)
    apply_k(s, p, coef, mask, 3)

    def to_w2(z, at, a0, a1):
        s0[at] = C0 * q0[at] + (C1 / SQ) * s0[at] + (C2 / SQ**2) * a0
        s1[at] = C0 * q1[at] + (C1 / SQ) * s1[at] + (C2 / SQ**2) * a1

    apply_k(p, None, coef, mask, 2, finish=to_w2)
    apply_k(s, p, coef, mask, 1)
    acc[...] = jnp.zeros((4, G, NX), f32)

    def to_w3(z, at, u3, _):
        to = block_rows(z)
        w, u1, u2 = we[at], q0[at], s0[at]
        v1_out[to] = u1
        v2_out[to] = u2
        v3_out[to] = u3
        for i, t in enumerate((r_ref[to] * w, w * u1, u1 * u2, u2 * u3)):
            acc[i] += t[:G] + t[G:]

    apply_k(p, None, coef, mask, 0, finish=to_w3)
    dots[...] = jnp.zeros((G, NX), f32)
    for i in range(4):
        dots[i : i + 1, :] = jnp.sum(acc[i], axis=0, keepdims=True)


def finish(x_ref, r_ref, w_ref, v1, v2, v3, dots, x_out, r_out):
    def total(i, scale):
        return jnp.sum(dots[i : i + 1, :], axis=1, keepdims=True) * (1.0 / scale)

    e0 = total(0, 1.0)
    g0 = total(1, SQ)
    h = total(2, SQ**2)
    k = total(3, SQ**3)
    a0 = e0 / g0
    e1 = a0 * a0 * h - e0
    beta = 1.0 + e1 / e0
    a1 = e1 / (beta * beta * g0 - 2.0 * beta * a0 * h + a0 * a0 * k)
    near = a0 + a1 * beta
    far = a1 * a0
    x_out[...] = x_ref[...] + near * w_ref[...] - (far * (1.0 / SQ)) * v2[...]
    r_out[...] = r_ref[...] - (near * (1.0 / SQ)) * v1[...] + (far * (1.0 / SQ**2)) * v3[...]


def all_sum(x):
    for axis in ("gx", "gy"):
        n = lax.axis_size(axis)
        copies = jnp.broadcast_to(x[None], (n, *x.shape))
        x = jnp.sum(lax.all_to_all(copies, axis, 0, 0), axis=0)
    return lax.psum(x, "gz")


def solve(right_side, initial, kappa_sq):
    flat = [v.reshape(NZ * NY, NX) for v in (initial, right_side, kappa_sq)]
    zdn, zup, ydn, yup = run(
        pack_block,
        [(LAYERS * NY, NX)] * 2 + [(MAIN_ROWS, NX)] * 2,
        [pltpu.with_memory_space_constraint(v, pltpu.HBM) for v in flat],
        scratch=[pltpu.VMEM((NZ * NY, NX), f32)] * 3 + [pltpu.SemaphoreType.DMA((3,))],
        space=pltpu.HBM,
    )
    zlo, zhi = exchange(zdn, zup, "gz")
    ylo, yhi = exchange(ydn, yup, "gy")
    down, up = run(pack_corners, [(CORNER_ROWS, NX)] * 2, (zlo, zhi))
    clo, chi = exchange(down, up, "gy")
    frame_shape = (FZ * FY, NX)
    xe, be, ke, down, up = run(frame, [frame_shape] * 3 + [(3 * Q_PACK, NX)] * 2, (*flat, zlo, zhi, ylo, yhi, clo, chi))
    xlo, xhi = exchange(down, up, "gx")
    tile = pltpu.VMEM(frame_shape, f32)
    block = (NZ * NY, NX)
    slab = (G * NY, NX)

    def stage1(xe, be_in, *rest):
        be = rest[-1]
        be[...] = be_in[...]
        first_stage(xe, be, *rest[:-1])

    r0, w0, zdn, zup, ydn, yup, c0, c1, m0, m1 = run(
        stage1,
        [block, block, slab, slab, (MAIN_ROWS2, NX), (MAIN_ROWS2, NX), frame_shape, frame_shape, frame_shape, frame_shape],
        (xe, be, ke, xlo, xhi),
        scratch=[tile] * 7,
    )
    zlo, zhi = exchange(zdn, zup, "gz")
    ylo, yhi = exchange(ydn, yup, "gy")
    down, up = run(pack_corners2, [(CORNER_ROWS2, NX)] * 2, (zlo, zhi))
    clo, chi = exchange(down, up, "gy")
    we, down, up = run(frame2, [frame_shape, (Q_PACK, NX), (Q_PACK, NX)], (w0, zlo, zhi, ylo, yhi, clo, chi))
    xlo, xhi = exchange(down, up, "gx")
    v1, v2, v3, dots = run(
        second_stage,
        [block, block, block, (G, NX)],
        (we, xlo, xhi, r0, c0, c1, m0, m1),
        scratch=[pltpu.VMEM((4, G, NX), f32)] + [tile] * 7,
    )
    dots = all_sum(dots)
    x, r = run(finish, [block, block], (flat[0], r0, w0, v1, v2, v3, dots))
    return x.reshape(NZ, NY, NX), r.reshape(NZ, NY, NX)


def solution(mesh):
    spec = P("gz", "gy", "gx")
    return jax.shard_map(solve, mesh=mesh, in_specs=(spec,) * 3, out_specs=(spec,) * 2, check_vma=False)
```

```python
import jax
import jax.numpy as jnp
from jax import lax
from jax.experimental import pallas as pl
from jax.experimental.pallas import tpu as pltpu
from jax.sharding import PartitionSpec as P

SWEEPS = 3
HIGH = 7.2
LOW = 0.072

NZ, NY, NX = 32, 16, 128
G = 8
FZ, FY = NZ + 2 * G, NY + 2 * G
DEPTHS = (6, 4, 7)
OFFS = (0, 6, 10)
LAYERS = 17
PIECES = [(f, t) for f in range(3) for t in range(1, DEPTHS[f] + 1)]
MAIN_ROWS = LAYERS * NZ


def place_corners(depths):
    sizes = [(d - t, f, t, side) for f, d in enumerate(depths) for t in range(1, d) for side in (0, 1)]
    free, at = [], {}
    for n, f, t, side in sorted(sizes, reverse=True):
        for i, used in enumerate(free):
            if used + n <= 8:
                break
        else:
            free.append(0)
            i = len(free) - 1
        at[f, t, side] = 8 * i + free[i]
        free[i] += n
    return at, 8 * len(free)


CORNERS, CORNER_ROWS = place_corners(DEPTHS)
CORNERS2, CORNER_ROWS2 = place_corners((G,))
MAIN_ROWS2 = G * NZ
Q_PACK = FZ // 16 * FY


def chebyshev():
    centre = (HIGH + LOW) / 2.0
    half = (HIGH - LOW) / 2.0
    sigma = centre / half
    rho = 1.0 / sigma
    d = [1.0 / centre, 0.0, 0.0]
    z = list(d)
    for _ in range(SWEEPS - 1):
        rho_new = 1.0 / (2.0 * sigma - rho)
        defect = [1.0, -z[0], -z[1]]
        d = [rho_new * rho * a + 2.0 * rho_new / half * b for a, b in zip(d, defect)]
        z = [a + b for a, b in zip(z, d)]
        rho = rho_new
    return z


C0, C1, C2 = chebyshev()
SQ = 36.0

f32 = jnp.float32
VM = pl.BlockSpec(memory_space=pltpu.VMEM)


def run(kernel, outs, args, scratch=(), mib=16, space=pltpu.VMEM):
    return pl.pallas_call(
        kernel,
        out_shape=[jax.ShapeDtypeStruct(s, f32) for s in outs],
        in_specs=[pl.BlockSpec(memory_space=space)] * len(args),
        out_specs=[VM] * len(outs),
        scratch_shapes=list(scratch),
        compiler_params=pltpu.CompilerParams(vmem_limit_bytes=mib << 20),
    )(*args)


def shift(x, axis, step):
    n = lax.axis_size(axis)
    pairs = [(i, i + step) for i in range(n) if 0 <= i + step < n]
    return lax.ppermute(x, axis, pairs)


def exchange(down, up, axis):
    from_above = shift(down, axis, -1)
    from_below = shift(up, axis, 1)
    return from_below, from_above


def swap(mine_a, mine_b, axis):
    n = lax.axis_size(axis)
    a = lax.ppermute(mine_a, axis, [(i, i ^ 1) for i in range(n)])
    b = lax.ppermute(mine_b, axis, [(i, i + 1 if i % 2 else i - 1) for i in range(1, n - 1)])
    return a, b


def is_even(axis):
    return lax.axis_index(axis) % 2 == 0


def place(even, dn, up):
    return jnp.where(even, up, dn), jnp.where(even, dn, up)


def sides(even, a, b):
    return jnp.where(even, b, a), jnp.where(even, a, b)


def pack_block(x_hbm, b_hbm, k_hbm, zdn, zup, ya, yb, x_ref, b_ref, k_ref, sems):
    fields = (x_ref, b_ref, k_ref)
    copies = [
        pltpu.make_async_copy(src, dst, sems.at[i])
        for i, (src, dst) in enumerate(zip((x_hbm, b_hbm, k_hbm), fields))
    ]
    for copy in copies:
        copy.start()
    for copy in copies:
        copy.wait()
    for f, field in enumerate(fields):
        n = DEPTHS[f] * NY
        at = OFFS[f] * NY
        zdn[at : at + n, :] = field[0:n, :]
        zup[at : at + n, :] = field[NZ * NY - n : NZ * NY, :]
    even = is_even("gy")
    for i, (f, t) in enumerate(PIECES):
        dn, up = (fields[f][pl.ds(row, NZ, stride=NY), :] for row in (t - 1, NY - t))
        ya[i * NZ : (i + 1) * NZ, :], yb[i * NZ : (i + 1) * NZ, :] = place(even, dn, up)


def pack_corners(lo_ref, hi_ref, a_ref, b_ref):
    even = is_even("gy")
    for f, t in PIECES:
        d, n = DEPTHS[f], DEPTHS[f] - t
        for side, ref, first in ((0, lo_ref, OFFS[f] + d - n), (1, hi_ref, OFFS[f])):
            if n:
                at = CORNERS[f, t, side]
                dn, up = (ref[pl.ds(first * NY + row, n, stride=NY), :] for row in (t - 1, NY - t))
                a_ref[at : at + n, :], b_ref[at : at + n, :] = place(even, dn, up)


def pack_lanes(read, a_ref, b_ref, base):
    group = lax.broadcasted_iota(jnp.int32, (FY, NX), 1) // G
    for q in range(FZ // 16):
        dn = jnp.zeros((FY, NX), f32)
        up = jnp.zeros((FY, NX), f32)
        for g in range(16):
            v = read(16 * q + g)
            a = v if g == 0 else pltpu.roll(v, G * g, 1)
            dn = jnp.where(group == g, a, dn)
            up = jnp.where(group == (g - 1) % 16, a, up)
        at = slice(base + q * FY, base + (q + 1) * FY)
        a_ref[at, :], b_ref[at, :] = place(is_even("gx"), dn, up)


def unpack_lanes(a_ref, b_ref, base, write):
    group = lax.broadcasted_iota(jnp.int32, (FY, NX), 1) // G
    for q in range(FZ // 16):
        at = slice(base + q * FY, base + (q + 1) * FY)
        lo, hi = sides(is_even("gx"), a_ref[at, :], b_ref[at, :])
        for g in range(16):
            v = jnp.where(group == g, hi, lo)
            write(16 * q + g, v if g == 0 else pltpu.roll(v, NX - G * g, 1))


def put_rows(out, t, first, n, lo_hi):
    for rows, row in zip(lo_hi, (G - t, G + NY + t - 1)):
        out[pl.ds(first * FY + row, n, stride=FY), :] = rows


def frame(x_ref, b_ref, k_ref, zlo, zhi, ya, yb, ca, cb, xe, be, ke, dn_ref, up_ref):
    even = is_even("gy")
    fields = (x_ref, b_ref, k_ref)
    for f, out in enumerate((xe, be, ke)):
        d = DEPTHS[f]
        out[...] = jnp.zeros((FZ * FY, NX), f32)
        for z in range(NZ):
            at = (G + z) * FY + G
            out[at : at + NY, :] = fields[f][z * NY : (z + 1) * NY, :]
        for j in range(d):
            src = (OFFS[f] + j) * NY
            at = (G - d + j) * FY + G
            out[at : at + NY, :] = zlo[src : src + NY, :]
            at = (G + NZ + j) * FY + G
            out[at : at + NY, :] = zhi[src : src + NY, :]
        for t in range(1, d + 1):
            i, n = OFFS[f] + t - 1, d - t
            put_rows(out, t, G, NZ, sides(even, ya[i * NZ : (i + 1) * NZ, :], yb[i * NZ : (i + 1) * NZ, :]))
            for side, first in ((0, G - n), (1, G + NZ)):
                if n:
                    at = CORNERS[f, t, side]
                    put_rows(out, t, first, n, sides(even, ca[at : at + n, :], cb[at : at + n, :]))
        pack_lanes(lambda z: out[z * FY : (z + 1) * FY, :], dn_ref, up_ref, f * Q_PACK)


PLANES = 8
GROUP = 4


class Window:
    def __init__(self, radius):
        self.first, self.last = G - radius, G + NZ + radius
        self.y, self.n = (G, NY) if radius == 0 else (4, 24) if radius <= 4 else (0, FY)

    def at(self, z, shift=0):
        return pl.ds(pl.multiple_of(z * FY, FY) + (self.y + shift), self.n)


def apply_k(src, dst, coef, mask, radius, finish=None):
    win = Window(radius)
    s0, s1 = src
    c0, c1 = coef
    m0, m1 = mask

    def group(planes):
        lane = lax.broadcasted_iota(jnp.int32, (win.n, NX), 1)
        here = [win.at(z) for z in planes]
        v0, v1 = [s0[at] for at in here], [s1[at] for at in here]
        left0 = [pltpu.roll(jnp.where(lane == NX - 1, b, a), 1, 1) for a, b in zip(v0, v1)]
        left1 = [pltpu.roll(jnp.where(lane == NX - 1, a, b), 1, 1) for a, b in zip(v0, v1)]
        right0 = [pltpu.roll(jnp.where(lane == 0, b, a), NX - 1, 1) for a, b in zip(v0, v1)]
        right1 = [pltpu.roll(jnp.where(lane == 0, a, b), NX - 1, 1) for a, b in zip(v0, v1)]

        def around(ref, z):
            y = ref[win.at(z, -1)] + ref[win.at(z, 1)]
            return y + (ref[win.at(z, -FY)] + ref[win.at(z, FY)])

        for i, z in enumerate(planes):
            at = here[i]
            r0 = c0[at] * v0[i] - m0[at] * (around(s0, z) + (left0[i] + right0[i]))
            r1 = c1[at] * v1[i] - m1[at] * (around(s1, z) + (left1[i] + right1[i]))
            if finish is None:
                dst[0][at] = r0
                dst[1][at] = r1
            else:
                finish(z, at, r0, r1)

    def some(z, n):
        for k in range(0, n, GROUP):
            group([z + k + i for i in range(min(GROUP, n - k))])

    count = win.last - win.first
    whole = count // PLANES

    def step(i, _):
        some(win.first + i * PLANES, PLANES)
        return 0

    lax.fori_loop(0, whole, step, 0)
    if count % PLANES:
        some(win.first + whole * PLANES, count % PLANES)


def block_rows(z):
    return pl.ds(pl.multiple_of((z - G) * NY, NY), NY)


def first_stage(xe, be, ke, lo, hi, r_out, w_out, zdn, zup, ya, yb, c0, c1, m0, m1, x1, b1, p0, p1, q0, q1):
    def put(ref):
        def write(z, v):
            ref[z * FY : (z + 1) * FY] = v

        return write

    def put_coef(z, k1):
        at = slice(z * FY, (z + 1) * FY)
        k0 = ke[at]
        c0[at] = 6.0 + k0
        c1[at] = 6.0 + k1
        m0[at] = jnp.where(k0 > 0.0, 1.0, 0.0)
        m1[at] = jnp.where(k1 > 0.0, 1.0, 0.0)

    unpack_lanes(lo, hi, 0, put(x1))
    unpack_lanes(lo, hi, Q_PACK, put(b1))
    unpack_lanes(lo, hi, 2 * Q_PACK, put_coef)
    coef, mask, p, q, b = (c0, c1), (m0, m1), (p0, p1), (q0, q1), (be, b1)

    apply_k((xe, x1), p, coef, mask, 5)

    def to_residual(z, at, v0, v1):
        be[at] = be[at] - v0 * (1.0 / SQ)
        b1[at] = b1[at] - v1 * (1.0 / SQ)

    apply_k(p, None, coef, mask, 4, finish=to_residual)
    apply_k(b, p, coef, mask, 3)
    apply_k(p, q, coef, mask, 2)
    apply_k(q, p, coef, mask, 1)

    def to_precond(z, at, v0, _):
        r = be[at]
        w_out[block_rows(z)] = C0 * r + (C1 / SQ) * q0[at] + (C2 / SQ**2) * v0
        r_out[block_rows(z)] = r

    apply_k(p, None, coef, mask, 0, finish=to_precond)
    zdn[...] = w_out[0 : G * NY]
    zup[...] = w_out[(NZ - G) * NY : NZ * NY]
    for t in range(1, G + 1):
        dn, up = (w_out[pl.ds(row, NZ, stride=NY), :] for row in (t - 1, NY - t))
        ya[(t - 1) * NZ : t * NZ, :], yb[(t - 1) * NZ : t * NZ, :] = place(is_even("gy"), dn, up)


def pack_corners2(lo_ref, hi_ref, a_ref, b_ref):
    even = is_even("gy")
    for t in range(1, G):
        n = G - t
        for side, ref, first in ((0, lo_ref, t), (1, hi_ref, 0)):
            at = CORNERS2[0, t, side]
            dn, up = (ref[pl.ds(first * NY + row, n, stride=NY), :] for row in (t - 1, NY - t))
            a_ref[at : at + n, :], b_ref[at : at + n, :] = place(even, dn, up)


def frame2(w_ref, zlo, zhi, ya, yb, ca, cb, we, dn_ref, up_ref):
    even = is_even("gy")
    for z in range(FZ):
        at = z * FY
        src, k = (zlo, z) if z < G else (w_ref, z - G) if z < G + NZ else (zhi, z - G - NZ)
        we[at + G : at + G + NY, :] = src[k * NY : (k + 1) * NY, :]
        if z < G or z >= G + NZ:
            we[at : at + G, :] = jnp.zeros((G, NX), f32)
            we[at + G + NY : at + FY, :] = jnp.zeros((G, NX), f32)
    for t in range(1, G + 1):
        n = G - t
        put_rows(we, t, G, NZ, sides(even, ya[(t - 1) * NZ : t * NZ, :], yb[(t - 1) * NZ : t * NZ, :]))
        for side, first in ((0, G - n), (1, G + NZ)):
            if n:
                at = CORNERS2[0, t, side]
                put_rows(we, t, first, n, sides(even, ca[at : at + n, :], cb[at : at + n, :]))
    pack_lanes(lambda z: we[z * FY : (z + 1) * FY, :], dn_ref, up_ref, 0)


def second_stage(we, lo, hi, r_ref, c0, c1, m0, m1, v1_out, v2_out, v3_out, dots, acc, w1, p0, p1, q0, q1, s0, s1):
    def write(z, v):
        w1[z * FY : (z + 1) * FY] = v

    unpack_lanes(lo, hi, 0, write)
    coef, mask, p, q, s = (c0, c1), (m0, m1), (p0, p1), (q0, q1), (s0, s1)
    apply_k((we, w1), p, coef, mask, 7)
    apply_k(p, q, coef, mask, 6)
    apply_k(q, p, coef, mask, 5)
    apply_k(p, s, coef, mask, 4)
    apply_k(s, p, coef, mask, 3)

    def to_w2(z, at, a0, a1):
        s0[at] = C0 * q0[at] + (C1 / SQ) * s0[at] + (C2 / SQ**2) * a0
        s1[at] = C0 * q1[at] + (C1 / SQ) * s1[at] + (C2 / SQ**2) * a1

    apply_k(p, None, coef, mask, 2, finish=to_w2)
    apply_k(s, p, coef, mask, 1)
    acc[...] = jnp.zeros((4, G, NX), f32)

    def to_w3(z, at, u3, _):
        to = block_rows(z)
        w, u1, u2 = we[at], q0[at], s0[at]
        v1_out[to] = u1
        v2_out[to] = u2
        v3_out[to] = u3
        for i, t in enumerate((r_ref[to] * w, w * u1, u1 * u2, u2 * u3)):
            acc[i] += t[:G] + t[G:]

    apply_k(p, None, coef, mask, 0, finish=to_w3)
    dots[...] = jnp.zeros((G, NX), f32)
    for i in range(4):
        dots[i : i + 1, :] = jnp.sum(acc[i], axis=0, keepdims=True)


def finish(x_ref, r_ref, w_ref, v1, v2, v3, dots, x_out, r_out):
    def total(i, scale):
        return jnp.sum(dots[i : i + 1, :], axis=1, keepdims=True) * (1.0 / scale)

    e0 = total(0, 1.0)
    g0 = total(1, SQ)
    h = total(2, SQ**2)
    k = total(3, SQ**3)
    a0 = e0 / g0
    e1 = a0 * a0 * h - e0
    beta = 1.0 + e1 / e0
    a1 = e1 / (beta * beta * g0 - 2.0 * beta * a0 * h + a0 * a0 * k)
    near = a0 + a1 * beta
    far = a1 * a0
    x_out[...] = x_ref[...] + near * w_ref[...] - (far * (1.0 / SQ)) * v2[...]
    r_out[...] = r_ref[...] - (near * (1.0 / SQ)) * v1[...] + (far * (1.0 / SQ**2)) * v3[...]


def all_sum(x):
    for axis in ("gx", "gy"):
        n = lax.axis_size(axis)
        copies = jnp.broadcast_to(x[None], (n, *x.shape))
        x = jnp.sum(lax.all_to_all(copies, axis, 0, 0), axis=0)
    return lax.psum(x, "gz")


def solve(right_side, initial, kappa_sq):
    flat = [v.reshape(NZ * NY, NX) for v in (initial, right_side, kappa_sq)]
    zdn, zup, ya, yb = run(
        pack_block,
        [(LAYERS * NY, NX)] * 2 + [(MAIN_ROWS, NX)] * 2,
        [pltpu.with_memory_space_constraint(v, pltpu.HBM) for v in flat],
        scratch=[pltpu.VMEM((NZ * NY, NX), f32)] * 3 + [pltpu.SemaphoreType.DMA((3,))],
        space=pltpu.HBM,
    )
    zlo, zhi = exchange(zdn, zup, "gz")
    ya, yb = swap(ya, yb, "gy")
    a, b = run(pack_corners, [(CORNER_ROWS, NX)] * 2, (zlo, zhi))
    ca, cb = swap(a, b, "gy")
    frame_shape = (FZ * FY, NX)
    xe, be, ke, a, b = run(frame, [frame_shape] * 3 + [(3 * Q_PACK, NX)] * 2, (*flat, zlo, zhi, ya, yb, ca, cb))
    xa, xb = swap(a, b, "gx")
    tile = pltpu.VMEM(frame_shape, f32)
    block = (NZ * NY, NX)
    slab = (G * NY, NX)

    def stage1(xe, be_in, *rest):
        be = rest[-1]
        be[...] = be_in[...]
        first_stage(xe, be, *rest[:-1])

    r0, w0, zdn, zup, ya, yb, c0, c1, m0, m1 = run(
        stage1,
        [block, block, slab, slab, (MAIN_ROWS2, NX), (MAIN_ROWS2, NX), frame_shape, frame_shape, frame_shape, frame_shape],
        (xe, be, ke, xa, xb),
        scratch=[tile] * 7,
    )
    zlo, zhi = exchange(zdn, zup, "gz")
    ya, yb = swap(ya, yb, "gy")
    a, b = run(pack_corners2, [(CORNER_ROWS2, NX)] * 2, (zlo, zhi))
    ca, cb = swap(a, b, "gy")
    we, a, b = run(frame2, [frame_shape, (Q_PACK, NX), (Q_PACK, NX)], (w0, zlo, zhi, ya, yb, ca, cb))
    xa, xb = swap(a, b, "gx")
    v1, v2, v3, dots = run(
        second_stage,
        [block, block, block, (G, NX)],
        (we, xa, xb, r0, c0, c1, m0, m1),
        scratch=[pltpu.VMEM((4, G, NX), f32)] + [tile] * 7,
    )
    dots = all_sum(dots)
    x, r = run(finish, [block, block], (flat[0], r0, w0, v1, v2, v3, dots))
    return x.reshape(NZ, NY, NX), r.reshape(NZ, NY, NX)


def solution(mesh):
    spec = P("gz", "gy", "gx")
    return jax.shard_map(solve, mesh=mesh, in_specs=(spec,) * 3, out_specs=(spec,) * 2, check_vma=False)
```

```python
import jax
import jax.numpy as jnp
from jax import lax
from jax.experimental import pallas as pl
from jax.experimental.pallas import tpu as pltpu
from jax.sharding import PartitionSpec as P

SWEEPS = 3
HIGH = 7.2
LOW = 0.072

NZ, NY, NX = 32, 16, 128
G = 8
FZ, FY = NZ + 2 * G, NY + 2 * G
DEPTHS = (6, 4, 7)
OFFS = (0, 6, 10)
LAYERS = 17
PIECES = [(f, t) for f in range(3) for t in range(1, DEPTHS[f] + 1)]
MAIN_ROWS = LAYERS * NZ


def place_corners(depths):
    sizes = [(d - t, f, t, side) for f, d in enumerate(depths) for t in range(1, d) for side in (0, 1)]
    free, at = [], {}
    for n, f, t, side in sorted(sizes, reverse=True):
        for i, used in enumerate(free):
            if used + n <= 8:
                break
        else:
            free.append(0)
            i = len(free) - 1
        at[f, t, side] = 8 * i + free[i]
        free[i] += n
    return at, 8 * len(free)


CORNERS, CORNER_ROWS = place_corners(DEPTHS)
CORNERS2, CORNER_ROWS2 = place_corners((G,))
MAIN_ROWS2 = G * NZ
Q_PACK = FZ // 16 * FY


def chebyshev():
    centre = (HIGH + LOW) / 2.0
    half = (HIGH - LOW) / 2.0
    sigma = centre / half
    rho = 1.0 / sigma
    d = [1.0 / centre, 0.0, 0.0]
    z = list(d)
    for _ in range(SWEEPS - 1):
        rho_new = 1.0 / (2.0 * sigma - rho)
        defect = [1.0, -z[0], -z[1]]
        d = [rho_new * rho * a + 2.0 * rho_new / half * b for a, b in zip(d, defect)]
        z = [a + b for a, b in zip(z, d)]
        rho = rho_new
    return z


C0, C1, C2 = chebyshev()
SQ = 36.0

f32 = jnp.float32
VM = pl.BlockSpec(memory_space=pltpu.VMEM)


def run(kernel, outs, args, scratch=(), mib=16, space=pltpu.VMEM):
    return pl.pallas_call(
        kernel,
        out_shape=[jax.ShapeDtypeStruct(s, f32) for s in outs],
        in_specs=[pl.BlockSpec(memory_space=space)] * len(args),
        out_specs=[VM] * len(outs),
        scratch_shapes=list(scratch),
        compiler_params=pltpu.CompilerParams(vmem_limit_bytes=mib << 20),
    )(*args)


def shift(x, axis, step):
    n = lax.axis_size(axis)
    pairs = [(i, i + step) for i in range(n) if 0 <= i + step < n]
    return lax.ppermute(x, axis, pairs)


def exchange(down, up, axis):
    from_above = shift(down, axis, -1)
    from_below = shift(up, axis, 1)
    return from_below, from_above


def swap(mine_a, mine_b, axis):
    n = lax.axis_size(axis)
    a = lax.ppermute(mine_a, axis, [(i, i ^ 1) for i in range(n)])
    b = lax.ppermute(mine_b, axis, [(i, i + 1 if i % 2 else i - 1) for i in range(1, n - 1)])
    return a, b


def is_even(axis):
    return lax.axis_index(axis) % 2 == 0


def place(even, dn, up):
    return jnp.where(even, up, dn), jnp.where(even, dn, up)


def sides(even, a, b):
    return jnp.where(even, b, a), jnp.where(even, a, b)


def pack_block(x_hbm, b_hbm, k_hbm, zdn, zup, ya, yb, x_ref, b_ref, k_ref, sems):
    fields = (x_ref, b_ref, k_ref)
    copies = [
        pltpu.make_async_copy(src, dst, sems.at[i])
        for i, (src, dst) in enumerate(zip((x_hbm, b_hbm, k_hbm), fields))
    ]
    for copy in copies:
        copy.start()
    for copy in copies:
        copy.wait()
    for f, field in enumerate(fields):
        n = DEPTHS[f] * NY
        at = OFFS[f] * NY
        zdn[at : at + n, :] = field[0:n, :]
        zup[at : at + n, :] = field[NZ * NY - n : NZ * NY, :]
    even = is_even("gy")
    for i, (f, t) in enumerate(PIECES):
        dn, up = (fields[f][pl.ds(row, NZ, stride=NY), :] for row in (t - 1, NY - t))
        ya[i * NZ : (i + 1) * NZ, :], yb[i * NZ : (i + 1) * NZ, :] = place(even, dn, up)


def pack_corners(lo_ref, hi_ref, a_ref, b_ref):
    even = is_even("gy")
    for f, t in PIECES:
        d, n = DEPTHS[f], DEPTHS[f] - t
        for side, ref, first in ((0, lo_ref, OFFS[f] + d - n), (1, hi_ref, OFFS[f])):
            if n:
                at = CORNERS[f, t, side]
                dn, up = (ref[pl.ds(first * NY + row, n, stride=NY), :] for row in (t - 1, NY - t))
                a_ref[at : at + n, :], b_ref[at : at + n, :] = place(even, dn, up)


def pack_lanes(read, a_ref, b_ref, base):
    group = lax.broadcasted_iota(jnp.int32, (FY, NX), 1) // G
    for q in range(FZ // 16):
        dn = jnp.zeros((FY, NX), f32)
        up = jnp.zeros((FY, NX), f32)
        for g in range(16):
            v = read(16 * q + g)
            a = v if g == 0 else pltpu.roll(v, G * g, 1)
            dn = jnp.where(group == g, a, dn)
            up = jnp.where(group == (g - 1) % 16, a, up)
        at = slice(base + q * FY, base + (q + 1) * FY)
        a_ref[at, :], b_ref[at, :] = place(is_even("gx"), dn, up)


def unpack_lanes(a_ref, b_ref, base, write):
    group = lax.broadcasted_iota(jnp.int32, (FY, NX), 1) // G
    for q in range(FZ // 16):
        at = slice(base + q * FY, base + (q + 1) * FY)
        lo, hi = sides(is_even("gx"), a_ref[at, :], b_ref[at, :])
        for g in range(16):
            v = jnp.where(group == g, hi, lo)
            write(16 * q + g, v if g == 0 else pltpu.roll(v, NX - G * g, 1))


def put_rows(out, t, first, n, lo_hi):
    for rows, row in zip(lo_hi, (G - t, G + NY + t - 1)):
        out[pl.ds(first * FY + row, n, stride=FY), :] = rows


def frame(x_ref, b_ref, k_ref, zlo, zhi, ya, yb, ca, cb, xe, be, ke, dn_ref, up_ref):
    even = is_even("gy")
    fields = (x_ref, b_ref, k_ref)
    for f, out in enumerate((xe, be, ke)):
        d = DEPTHS[f]
        out[...] = jnp.zeros((FZ * FY, NX), f32)
        for z in range(NZ):
            at = (G + z) * FY + G
            out[at : at + NY, :] = fields[f][z * NY : (z + 1) * NY, :]
        for j in range(d):
            src = (OFFS[f] + j) * NY
            at = (G - d + j) * FY + G
            out[at : at + NY, :] = zlo[src : src + NY, :]
            at = (G + NZ + j) * FY + G
            out[at : at + NY, :] = zhi[src : src + NY, :]
        for t in range(1, d + 1):
            i, n = OFFS[f] + t - 1, d - t
            put_rows(out, t, G, NZ, sides(even, ya[i * NZ : (i + 1) * NZ, :], yb[i * NZ : (i + 1) * NZ, :]))
            for side, first in ((0, G - n), (1, G + NZ)):
                if n:
                    at = CORNERS[f, t, side]
                    put_rows(out, t, first, n, sides(even, ca[at : at + n, :], cb[at : at + n, :]))
        pack_lanes(lambda z: out[z * FY : (z + 1) * FY, :], dn_ref, up_ref, f * Q_PACK)


TRIPS = 1
GROUP = 1


class Window:
    def __init__(self, radius):
        self.first, self.last = G - radius, G + NZ + radius
        self.y, self.n = (G, NY) if radius == 0 else (4, 24) if radius <= 4 else (0, FY)

    def at(self, z, shift=0):
        return pl.ds(pl.multiple_of(z * FY, FY) + (self.y + shift), self.n)


def apply_k(src, dst, coef, mask, radius, finish=None):
    win = Window(radius)
    s0, s1 = src
    c0, c1 = coef
    m0, m1 = mask

    def group(planes):
        lane = lax.broadcasted_iota(jnp.int32, (win.n, NX), 1)
        here = [win.at(z) for z in planes]
        v0, v1 = [s0[at] for at in here], [s1[at] for at in here]
        left0 = [pltpu.roll(jnp.where(lane == NX - 1, b, a), 1, 1) for a, b in zip(v0, v1)]
        left1 = [pltpu.roll(jnp.where(lane == NX - 1, a, b), 1, 1) for a, b in zip(v0, v1)]
        right0 = [pltpu.roll(jnp.where(lane == 0, b, a), NX - 1, 1) for a, b in zip(v0, v1)]
        right1 = [pltpu.roll(jnp.where(lane == 0, a, b), NX - 1, 1) for a, b in zip(v0, v1)]

        def around(ref, z):
            y = ref[win.at(z, -1)] + ref[win.at(z, 1)]
            return y + (ref[win.at(z, -FY)] + ref[win.at(z, FY)])

        for i, z in enumerate(planes):
            at = here[i]
            r0 = c0[at] * v0[i] - m0[at] * (around(s0, z) + (left0[i] + right0[i]))
            r1 = c1[at] * v1[i] - m1[at] * (around(s1, z) + (left1[i] + right1[i]))
            if finish is None:
                dst[0][at] = r0
                dst[1][at] = r1
            else:
                finish(z, at, r0, r1)

    def some(z, n):
        for k in range(0, n, GROUP):
            group([z + k + i for i in range(min(GROUP, n - k))])

    planes = (win.last - win.first) // TRIPS

    def step(i, _):
        some(win.first + i * planes, planes)
        return 0

    lax.fori_loop(0, TRIPS, step, 0)


def block_rows(z):
    return pl.ds(pl.multiple_of((z - G) * NY, NY), NY)


def first_stage(xe, be, ke, lo, hi, r_out, w_out, zdn, zup, ya, yb, c0, c1, m0, m1, x1, b1, p0, p1, q0, q1):
    def put(ref):
        def write(z, v):
            ref[z * FY : (z + 1) * FY] = v

        return write

    def put_coef(z, k1):
        at = slice(z * FY, (z + 1) * FY)
        k0 = ke[at]
        c0[at] = 6.0 + k0
        c1[at] = 6.0 + k1
        m0[at] = jnp.where(k0 > 0.0, 1.0, 0.0)
        m1[at] = jnp.where(k1 > 0.0, 1.0, 0.0)

    unpack_lanes(lo, hi, 0, put(x1))
    unpack_lanes(lo, hi, Q_PACK, put(b1))
    unpack_lanes(lo, hi, 2 * Q_PACK, put_coef)
    coef, mask, p, q, b = (c0, c1), (m0, m1), (p0, p1), (q0, q1), (be, b1)

    apply_k((xe, x1), p, coef, mask, 5)

    def to_residual(z, at, v0, v1):
        be[at] = be[at] - v0 * (1.0 / SQ)
        b1[at] = b1[at] - v1 * (1.0 / SQ)

    apply_k(p, None, coef, mask, 4, finish=to_residual)
    apply_k(b, p, coef, mask, 3)
    apply_k(p, q, coef, mask, 2)
    apply_k(q, p, coef, mask, 1)

    def to_precond(z, at, v0, _):
        r = be[at]
        w_out[block_rows(z)] = C0 * r + (C1 / SQ) * q0[at] + (C2 / SQ**2) * v0
        r_out[block_rows(z)] = r

    apply_k(p, None, coef, mask, 0, finish=to_precond)
    zdn[...] = w_out[0 : G * NY]
    zup[...] = w_out[(NZ - G) * NY : NZ * NY]
    for t in range(1, G + 1):
        dn, up = (w_out[pl.ds(row, NZ, stride=NY), :] for row in (t - 1, NY - t))
        ya[(t - 1) * NZ : t * NZ, :], yb[(t - 1) * NZ : t * NZ, :] = place(is_even("gy"), dn, up)


def pack_corners2(lo_ref, hi_ref, a_ref, b_ref):
    even = is_even("gy")
    for t in range(1, G):
        n = G - t
        for side, ref, first in ((0, lo_ref, t), (1, hi_ref, 0)):
            at = CORNERS2[0, t, side]
            dn, up = (ref[pl.ds(first * NY + row, n, stride=NY), :] for row in (t - 1, NY - t))
            a_ref[at : at + n, :], b_ref[at : at + n, :] = place(even, dn, up)


def frame2(w_ref, zlo, zhi, ya, yb, ca, cb, we, dn_ref, up_ref):
    even = is_even("gy")
    for z in range(FZ):
        at = z * FY
        src, k = (zlo, z) if z < G else (w_ref, z - G) if z < G + NZ else (zhi, z - G - NZ)
        we[at + G : at + G + NY, :] = src[k * NY : (k + 1) * NY, :]
        if z < G or z >= G + NZ:
            we[at : at + G, :] = jnp.zeros((G, NX), f32)
            we[at + G + NY : at + FY, :] = jnp.zeros((G, NX), f32)
    for t in range(1, G + 1):
        n = G - t
        put_rows(we, t, G, NZ, sides(even, ya[(t - 1) * NZ : t * NZ, :], yb[(t - 1) * NZ : t * NZ, :]))
        for side, first in ((0, G - n), (1, G + NZ)):
            if n:
                at = CORNERS2[0, t, side]
                put_rows(we, t, first, n, sides(even, ca[at : at + n, :], cb[at : at + n, :]))
    pack_lanes(lambda z: we[z * FY : (z + 1) * FY, :], dn_ref, up_ref, 0)


def second_stage(we, lo, hi, r_ref, c0, c1, m0, m1, v1_out, v2_out, v3_out, dots, acc, w1, p0, p1, q0, q1, s0, s1):
    def write(z, v):
        w1[z * FY : (z + 1) * FY] = v

    unpack_lanes(lo, hi, 0, write)
    coef, mask, p, q, s = (c0, c1), (m0, m1), (p0, p1), (q0, q1), (s0, s1)
    apply_k((we, w1), p, coef, mask, 7)
    apply_k(p, q, coef, mask, 6)
    apply_k(q, p, coef, mask, 5)
    apply_k(p, s, coef, mask, 4)
    apply_k(s, p, coef, mask, 3)

    def to_w2(z, at, a0, a1):
        s0[at] = C0 * q0[at] + (C1 / SQ) * s0[at] + (C2 / SQ**2) * a0
        s1[at] = C0 * q1[at] + (C1 / SQ) * s1[at] + (C2 / SQ**2) * a1

    apply_k(p, None, coef, mask, 2, finish=to_w2)
    apply_k(s, p, coef, mask, 1)
    acc[...] = jnp.zeros((4, G, NX), f32)

    def to_w3(z, at, u3, _):
        to = block_rows(z)
        w, u1, u2 = we[at], q0[at], s0[at]
        v1_out[to] = u1
        v2_out[to] = u2
        v3_out[to] = u3
        for i, t in enumerate((r_ref[to] * w, w * u1, u1 * u2, u2 * u3)):
            acc[i] += t[:G] + t[G:]

    apply_k(p, None, coef, mask, 0, finish=to_w3)
    dots[...] = jnp.zeros((G, NX), f32)
    for i in range(4):
        dots[i : i + 1, :] = jnp.sum(acc[i], axis=0, keepdims=True)


def finish(x_ref, r_ref, w_ref, v1, v2, v3, dots, x_out, r_out):
    def lanes(i, scale):
        return dots[i : i + 1, :] * (1.0 / scale)

    def total(v):
        return jnp.sum(v, axis=1, keepdims=True)

    e, g, h, k = (lanes(i, SQ**i) for i in range(4))
    e0 = total(e)
    a0 = e0 / total(g)
    e1 = total(e - a0 * (2.0 * g - a0 * h))
    beta = 1.0 + e1 / e0
    a1 = e1 / total(beta * beta * g - a0 * (2.0 * beta * h - a0 * k))
    near = a0 + a1 * beta
    far = a1 * a0
    x_out[...] = x_ref[...] + near * w_ref[...] - (far * (1.0 / SQ)) * v2[...]
    r_out[...] = r_ref[...] - (near * (1.0 / SQ)) * v1[...] + (far * (1.0 / SQ**2)) * v3[...]


def all_sum(x):
    for axis in ("gx", "gy"):
        n = lax.axis_size(axis)
        copies = jnp.broadcast_to(x[None], (n, *x.shape))
        x = jnp.sum(lax.all_to_all(copies, axis, 0, 0), axis=0)
    return lax.psum(x, "gz")


def solve(right_side, initial, kappa_sq):
    flat = [v.reshape(NZ * NY, NX) for v in (initial, right_side, kappa_sq)]
    zdn, zup, ya, yb = run(
        pack_block,
        [(LAYERS * NY, NX)] * 2 + [(MAIN_ROWS, NX)] * 2,
        [pltpu.with_memory_space_constraint(v, pltpu.HBM) for v in flat],
        scratch=[pltpu.VMEM((NZ * NY, NX), f32)] * 3 + [pltpu.SemaphoreType.DMA((3,))],
        space=pltpu.HBM,
    )
    zlo, zhi = exchange(zdn, zup, "gz")
    ya, yb = swap(ya, yb, "gy")
    a, b = run(pack_corners, [(CORNER_ROWS, NX)] * 2, (zlo, zhi))
    ca, cb = swap(a, b, "gy")
    frame_shape = (FZ * FY, NX)
    xe, be, ke, a, b = run(frame, [frame_shape] * 3 + [(3 * Q_PACK, NX)] * 2, (*flat, zlo, zhi, ya, yb, ca, cb))
    xa, xb = swap(a, b, "gx")
    tile = pltpu.VMEM(frame_shape, f32)
    block = (NZ * NY, NX)
    slab = (G * NY, NX)

    def stage1(xe, be_in, *rest):
        be = rest[-1]
        be[...] = be_in[...]
        first_stage(xe, be, *rest[:-1])

    r0, w0, zdn, zup, ya, yb, c0, c1, m0, m1 = run(
        stage1,
        [block, block, slab, slab, (MAIN_ROWS2, NX), (MAIN_ROWS2, NX), frame_shape, frame_shape, frame_shape, frame_shape],
        (xe, be, ke, xa, xb),
        scratch=[tile] * 7,
    )
    zlo, zhi = exchange(zdn, zup, "gz")
    ya, yb = swap(ya, yb, "gy")
    a, b = run(pack_corners2, [(CORNER_ROWS2, NX)] * 2, (zlo, zhi))
    ca, cb = swap(a, b, "gy")
    we, a, b = run(frame2, [frame_shape, (Q_PACK, NX), (Q_PACK, NX)], (w0, zlo, zhi, ya, yb, ca, cb))
    xa, xb = swap(a, b, "gx")
    v1, v2, v3, dots = run(
        second_stage,
        [block, block, block, (G, NX)],
        (we, xa, xb, r0, c0, c1, m0, m1),
        scratch=[pltpu.VMEM((4, G, NX), f32)] + [tile] * 7,
    )
    dots = all_sum(dots)
    x, r = run(finish, [block, block], (flat[0], r0, w0, v1, v2, v3, dots))
    return x.reshape(NZ, NY, NX), r.reshape(NZ, NY, NX)


def solution(mesh):
    spec = P("gz", "gy", "gx")
    return jax.shard_map(solve, mesh=mesh, in_specs=(spec,) * 3, out_specs=(spec,) * 2, check_vma=False)
```
